512 devices in a mesh: ctx: 64 (over x, z), head: 8 (over y, core).
Axes of the slice: x: 4, y: 4, z: 16, core: 2. Of those that a mesh axis runs over, the one named last changes fastest.
Arguments:
- prefix_len: int32 [2], replicated, may hold values from 2048 to 16384, as said below
- page_slot: int32 [2, 64], replicated, may hold values from 0 to 127, as said below
- queries: bfloat16 [512, 8192], P('ctx', 'head'), may hold values from -6 to 6
- new_kv: bfloat16 [2, 512, 1024], P(None, 'ctx', 'head'), may hold values from -6 to 6
- cache: bfloat16 [2, 128, 256, 1024], P(None, 'ctx', None, 'head'), may hold values from -6 to 6
Outputs:
- attention: bfloat16 [512, 8192], P(('ctx', 'head'))
The draws below stay inside these ranges and needn't reach their ends.
Inputs may be any that keep to these rules, and one draw needn't show every extreme that they name: `prefix_len`: each conversation's prefix holds 2048 to 16384 tokens; one conversation holds exactly 16384. `page_slot`: every slot number appears once; slot s lies at ctx index s // 2, as its slot s % 2.
All inputs are finite; a program needn't handle non-finite values.
Results may differ from the reference program's by a relative error of at most 0.0075.
Values may be sent and summed in bfloat16 or wider, within the bound.
A program may use at most 64 MiB of HBM per device.

```python
import jax
import jax.numpy as jnp

HEADS = 64
KV_HEADS = 8
HEAD_DIM = 128
CONVS = 2
SPAN = 256
PAGE = 256
MAXLEN = 16384
MINLEN = 2048
MAXPAGES = 64
ROWS = 512


def slot_table(key):
    base_key = jax.random.fold_in(key, 11)
    dialog_rank = jax.random.permutation(jax.random.fold_in(base_key, 1), CONVS).astype(jnp.int32)
    page_ids = jnp.arange(MAXPAGES, dtype=jnp.int32)
    order_score = dialog_rank[:, None] * MAXPAGES + page_ids[None, :]
    jitter = jax.random.randint(jax.random.fold_in(base_key, 2), (CONVS, MAXPAGES), 0, max(MAXPAGES // 2, 1))
    item_count = CONVS * MAXPAGES
    sort_score = (order_score + jitter) * item_count + jnp.arange(item_count, dtype=jnp.int32).reshape(CONVS, MAXPAGES)
    sorted_items = jnp.argsort(sort_score.reshape(-1), stable=True)
    return jnp.argsort(sorted_items, stable=True).astype(jnp.int32).reshape(CONVS, MAXPAGES)


def draw_page_slot(key, part):
    return slot_table(key)


def draw_prefix_len(key, part):
    length_key = jax.random.fold_in(key, 31)
    drawn = jax.random.randint(jax.random.fold_in(length_key, 1), (CONVS,), MINLEN, MAXLEN + 1)
    longest = jax.random.randint(jax.random.fold_in(length_key, 2), (), 0, CONVS)
    shortest = (longest + 1 + jax.random.randint(jax.random.fold_in(length_key, 3), (), 0, max(CONVS - 1, 1))) % CONVS
    dialog_ids = jnp.arange(CONVS, dtype=jnp.int32)
    drawn = jnp.where(dialog_ids == shortest, MINLEN, drawn)
    drawn = jnp.where(dialog_ids == longest, MAXLEN, drawn)
    return drawn.astype(jnp.int32)


def draw_queries(key, part):
    array_shape = (CONVS * SPAN, HEADS * HEAD_DIM)
    value_key = jax.random.fold_in(key, 41)
    drawn = jnp.clip(jax.random.normal(value_key, array_shape, jnp.float32), -5.5, 5.5)
    return drawn.astype(jnp.bfloat16)


def draw_cache(key, part):
    array_shape = (2, CONVS * MAXPAGES, PAGE, KV_HEADS * HEAD_DIM)
    value_key = jax.random.fold_in(key, 53)
    drawn = jnp.clip(jax.random.normal(value_key, array_shape, jnp.float32), -5.5, 5.5)
    return drawn.astype(jnp.bfloat16)


def block_scale(own_key, shape, shards, least, top_value):
    gain, own = 1.0, jax.random.fold_in(own_key, 6)
    for axis_at, parts in shards:
        draws = jnp.exp(jax.random.uniform(jax.random.fold_in(own, axis_at), (parts,), jnp.float32, least / len(shards), top_value / len(shards)))
        gain = gain * jnp.repeat(draws, shape[axis_at] // parts).reshape([-1 if axis == axis_at else 1 for axis in range(len(shape))])
    return gain


def bell_draw(own_key, dims, deviation, reach, shards=(), held_as=jnp.bfloat16):
    values = jax.random.normal(own_key, dims, jnp.float32) * deviation
    if len(shards) > 0:
        values = block_scale(own_key, dims, shards, -0.22, 0.18) * values
    return jnp.clip(values, min=-reach, max=reach).astype(held_as)


def setup_inputs(seed: int = 0) -> dict:
    keys = jax.random.split(jax.random.key(seed), 6)
    prefix_len = draw_prefix_len(jax.random.fold_in(keys[5], 71), 0)
    page_slot = draw_page_slot(jax.random.fold_in(keys[5], 71), 0)
    queries = draw_queries(jax.random.fold_in(keys[5], 71), 0)
    new_kv = bell_draw(keys[3], (2, ROWS, KV_HEADS * HEAD_DIM), 1.0, 6.0, ((1, 64), (2, 8)))
    cache = draw_cache(jax.random.fold_in(keys[5], 71), 0)
    return dict(prefix_len=prefix_len, page_slot=page_slot, queries=queries, new_kv=new_kv, cache=cache)


MASKED = -1.0e30


def reference(prefix_len, page_slot, queries, new_kv, cache):
    score_scale = HEAD_DIM ** -0.5
    group_size = HEADS // KV_HEADS
    outputs = []
    for dialog in range(CONVS):
        slot_list = page_slot[dialog]
        prefix_keys = jnp.take(cache[0], slot_list, axis=0).reshape(MAXLEN, KV_HEADS * HEAD_DIM)
        prefix_values = jnp.take(cache[1], slot_list, axis=0).reshape(MAXLEN, KV_HEADS * HEAD_DIM)
        row_start = dialog * SPAN
        all_keys = jnp.concatenate([prefix_keys, new_kv[0, row_start:row_start + SPAN]], axis=0)
        all_values = jnp.concatenate([prefix_values, new_kv[1, row_start:row_start + SPAN]], axis=0)
        positions = jnp.arange(MAXLEN + SPAN, dtype=jnp.int32)
        turn_steps = jnp.arange(SPAN, dtype=jnp.int32)
        live_keys = jnp.where(positions[None, :] < MAXLEN,
                              positions[None, :] < prefix_len[dialog],
                              positions[None, :] - MAXLEN <= turn_steps[:, None])
        query_rows = queries[row_start:row_start + SPAN]
        pieces = []
        for kv_group in range(KV_HEADS):
            query_block = query_rows[:, kv_group * group_size * HEAD_DIM:(kv_group + 1) * group_size * HEAD_DIM]
            query_block = query_block.reshape(SPAN * group_size, HEAD_DIM)
            key_block = all_keys[:, kv_group * HEAD_DIM:(kv_group + 1) * HEAD_DIM]
            value_block = all_values[:, kv_group * HEAD_DIM:(kv_group + 1) * HEAD_DIM]
            scores = jnp.dot(query_block, key_block.T, preferred_element_type=jnp.float32) * score_scale
            scores = scores.reshape(SPAN, group_size, MAXLEN + SPAN)
            scores = jnp.where(live_keys[:, None, :], scores, MASKED)
            row_top = jnp.max(scores, axis=2, keepdims=True)
            weights = jnp.exp(scores - row_top).astype(jnp.bfloat16)
            totals = jnp.sum(weights.astype(jnp.float32), axis=2)
            mixed = jnp.dot(weights.reshape(SPAN * group_size, MAXLEN + SPAN), value_block,
                            preferred_element_type=jnp.float32).reshape(SPAN, group_size, HEAD_DIM)
            pieces.append((mixed / totals[..., None]).reshape(SPAN, group_size * HEAD_DIM))
        outputs.append(jnp.concatenate(pieces, axis=1))
    return jnp.concatenate(outputs, axis=0).astype(jnp.bfloat16)
```

```python
import functools

import jax
import jax.numpy as jnp
from jax import lax
from jax.experimental import pallas as pl
from jax.experimental.pallas import tpu as pltpu
from jax.sharding import PartitionSpec as P

HEAD_DIM = 128
PAGE = 256
SLOTS = 2
XS = 4
MASKED = -1e30
FLOOR = -1e20
LOG2E = 1.4426950408889634
MESH = pl.DeviceIdType.MESH
F32 = jnp.float32
BF16 = jnp.bfloat16


def exchange(copies):
    for copy in copies:
        copy.start()
    return copies


def kernel(
    zs, hs, rows, group, lens_ref, slot_ref, q_ref, new_ref, cache_ref, out_ref,
    kv_all, new_all, q_all, part, part_stat, got, got_stat, bias, fin, heads,
    kv_send, kv_recv, new_send, new_recv, q_send, q_recv,
    part_send, part_recv, stat_send, stat_recv, head_send, head_recv, own_sem,
):
    ctx = lax.axis_index("ctx")
    head = lax.axis_index("head")
    x, z = ctx // zs, ctx % zs
    side = x // (XS // 2)
    block = rows * group
    per = rows // hs * group

    def at_x(k):
        return (lax.rem(x + k, XS) * zs + z, head)

    def at_z(there):
        return (x * zs + there, head)

    own_kv = pltpu.make_async_copy(cache_ref, kv_all.at[x], own_sem)
    own_kv.start()

    barrier = pltpu.get_barrier_semaphore()
    for k in range(1, XS):
        pl.semaphore_signal(barrier, inc=1, device_id=at_x(k), device_id_type=MESH)
    for k in range(1, zs):
        pl.semaphore_signal(barrier, inc=1, device_id=at_z(lax.rem(z + k, zs)), device_id_type=MESH)
    for k in range(1, hs):
        pl.semaphore_signal(
            barrier, inc=1, device_id=(ctx, lax.rem(head + k, hs)), device_id_type=MESH
        )

    queries = q_ref[...].astype(F32)
    queries = jnp.concatenate(
        [queries[:, h * HEAD_DIM:(h + 1) * HEAD_DIM] for h in range(group)], axis=0
    )
    q_all[z] = queries.astype(BF16)
    new_all[x] = new_ref[...]

    pl.semaphore_wait(barrier, XS - 1 + zs - 1 + hs - 1)

    kv_copies = exchange([
        pltpu.make_async_remote_copy(
            cache_ref, kv_all.at[x], kv_send.at[k], kv_recv.at[x],
            device_id=at_x(k), device_id_type=MESH,
        )
        for k in (2, 1, 3)
    ])
    q_copies = exchange([
        pltpu.make_async_remote_copy(
            q_all.at[z], q_all.at[z], q_send.at[k], q_recv.at[z],
            device_id=at_z(lax.rem(z + k, zs)), device_id_type=MESH,
        )
        for k in sorted(range(1, zs), key=lambda k: -min(k, zs - k))
    ])
    new_copies = exchange([
        pltpu.make_async_remote_copy(
            new_ref, new_all.at[x], new_send.at[k], new_recv.at[x],
            device_id=at_x(k), device_id_type=MESH,
        )
        for k in (2, 1, 3)
    ])

    pages = slot_ref.shape[1]
    table = slot_ref[pl.ds(side, 1), :]
    page_ids = lax.broadcasted_iota(jnp.int32, (1, pages), 1)
    live = jnp.clip(lens_ref[side] - page_ids * PAGE, 0, PAGE).astype(F32)
    slots = lax.broadcasted_iota(jnp.int32, (XS * SLOTS, pages), 0)
    slots = SLOTS * (slots // SLOTS * zs + z) + slots % SLOTS
    live = jnp.sum(jnp.where(table == slots, live, 0.0), axis=1, keepdims=True)
    offsets = lax.broadcasted_iota(jnp.int32, (XS * SLOTS, PAGE), 1).astype(F32)
    bias[...] = jnp.where(offsets < live, 0.0, MASKED)

    own_kv.wait()

    def wait_from(dst, send, recv, index):
        pltpu.make_async_remote_copy(
            dst.at[index], dst.at[index], send, recv.at[index],
            device_id=(ctx, head), device_id_type=MESH,
        ).wait_recv()

    for k in range(1, zs):
        wait_from(q_all, q_send.at[k], q_recv, lax.rem(z + k, zs))
    for k in range(1, XS):
        wait_from(new_all, new_send.at[k], new_recv, lax.rem(x + k, XS))
        wait_from(kv_all, kv_send.at[k], kv_recv, lax.rem(x + k, XS))

    new_keys = jnp.concatenate([new_all[i, 0].astype(F32) for i in range(XS)], axis=0).astype(BF16)
    new_values = jnp.concatenate([new_all[i, 1].astype(F32) for i in range(XS)], axis=0).astype(BF16)
    fresh = XS * rows
    new_at = lax.broadcasted_iota(jnp.int32, (2 * block, fresh), 1)
    new_rows = rows * (new_at // rows * zs + z) + new_at % rows
    at = lax.broadcasted_iota(jnp.int32, (2 * block, fresh), 0)
    scale = HEAD_DIM ** (-0.5) * LOG2E
    contract = (((1,), (1,)), ((), ()))
    ones = jnp.ones((SLOTS * PAGE, HEAD_DIM), BF16)
    diagonal = (
        lax.broadcasted_iota(jnp.int32, (block, HEAD_DIM), 0)
        == lax.broadcasted_iota(jnp.int32, (block, HEAD_DIM), 1)
    )

    def part_copy(there):
        return pltpu.make_async_remote_copy(
            part.at[there], got.at[z], part_send.at[there], part_recv.at[z],
            device_id=at_z(there), device_id_type=MESH,
        )

    def stat_copy(there):
        return pltpu.make_async_remote_copy(
            part_stat.at[there], got_stat.at[z], stat_send.at[there], stat_recv.at[z],
            device_id=at_z(there), device_id_type=MESH,
        )

    def pair_step(step, carry):
        pair = lax.rem(z // 2 + zs // 4 + step, zs // 2)
        first = pair * 2
        mine = q_all[pl.ds(first, 2)].reshape(2 * block, HEAD_DIM)
        scores = []
        for i in range(XS):
            keys = kv_all[i, 0].reshape(SLOTS * PAGE, HEAD_DIM)
            raw = lax.dot_general(mine, keys, contract, preferred_element_type=F32)
            masks = jnp.concatenate(
                [bias[SLOTS * i + j:SLOTS * i + j + 1, :] for j in range(SLOTS)], axis=1
            )
            scores.append(raw * scale + masks)
        raw = lax.dot_general(mine, new_keys, contract, preferred_element_type=F32)
        q_rows = rows * (x * zs + first + at // block) + at % rows
        seen = (new_rows <= q_rows) & (new_rows >= side * (XS // 2 * zs * rows))
        scores.append(jnp.where(seen, raw * scale, MASKED))
        tops = [jnp.max(s, axis=1, keepdims=True) for s in scores]
        top = functools.reduce(jnp.maximum, tops, jnp.full((2 * block, 1), FLOOR, F32))
        total = jnp.zeros((2 * block, 2 * HEAD_DIM), F32)
        for i in range(XS):
            weights = jnp.exp2(scores[i] - top).astype(BF16)
            values = kv_all[i, 1].reshape(SLOTS * PAGE, HEAD_DIM)
            total += jnp.dot(
                weights, jnp.concatenate([values, ones], axis=1), preferred_element_type=F32
            )
        weights = jnp.exp2(scores[XS] - top).astype(BF16)
        total += jnp.dot(
            weights, jnp.concatenate([new_values, ones[:fresh]], axis=1), preferred_element_type=F32
        )
        amount = total[:, HEAD_DIM:]
        full = jnp.maximum(amount, 1.0)
        normal = (total[:, :HEAD_DIM] / full).astype(BF16)
        stat = jnp.where(amount > 0.0, top + jnp.log2(full), MASKED)
        for j in range(2):
            part[first + j] = normal[j * block:(j + 1) * block]
            part_stat[first + j] = jnp.sum(
                jnp.where(diagonal, stat[j * block:(j + 1) * block], 0.0), axis=0, keepdims=True
            )
        for j in range(2):
            @pl.when(first + j != z)
            def _():
                part_copy(first + j).start()
                stat_copy(first + j).start()
        return carry

    lax.fori_loop(0, zs // 2, pair_step, 0)
    got[z] = part[z]
    got_stat[z] = part_stat[z]
    for k in range(1, zs):
        there = lax.rem(z + k, zs)
        wait_from(got_stat, stat_send.at[there], stat_recv, there)
        wait_from(got, part_send.at[there], part_recv, there)

    stats = [got_stat[i] for i in range(zs)]
    top = functools.reduce(jnp.maximum, stats)
    shares = [jnp.exp2(s - top) for s in stats]
    share_sum = functools.reduce(jnp.add, shares)
    merged = jnp.zeros((block, HEAD_DIM), F32)
    for i in range(zs):
        share = jnp.broadcast_to(shares[i] / share_sum, (block, HEAD_DIM))
        share = jnp.sum(jnp.where(diagonal, share, 0.0), axis=1, keepdims=True)
        merged += share * got[i].astype(F32)
    for h in range(group):
        fin[pl.ds(h, rows, stride=group), :] = merged[h * rows:(h + 1) * rows]

    def fin_at(there):
        return fin.at[pl.ds(pl.multiple_of(there * per, 8), per), :]

    head_copies = exchange([
        pltpu.make_async_remote_copy(
            fin_at(lax.rem(head + k, hs)), heads.at[head], head_send.at[k], head_recv.at[head],
            device_id=(ctx, lax.rem(head + k, hs)), device_id_type=MESH,
        )
        for k in range(1, hs)
    ])
    heads[head] = fin[pl.ds(pl.multiple_of(head * per, 8), per), :]
    for k in range(1, hs):
        wait_from(heads, head_send.at[k], head_recv, lax.rem(head + k, hs))
    out_ref[...] = heads[...]
    for copy in kv_copies + q_copies + new_copies + head_copies:
        copy.wait_send()
    for k in range(1, zs):
        there = lax.rem(z + k, zs)
        part_copy(there).wait_send()
        stat_copy(there).wait_send()


def local(zs, hs, prefix_len, page_slot, queries, new_kv, cache):
    rows = queries.shape[0]
    group = queries.shape[1] // HEAD_DIM
    block = rows * group
    per = rows // hs * group
    dma = pltpu.SemaphoreType.DMA
    result = pl.pallas_call(
        functools.partial(kernel, zs, hs, rows, group),
        out_shape=jax.ShapeDtypeStruct((hs, per, HEAD_DIM), F32),
        in_specs=[
            pl.BlockSpec(memory_space=pltpu.SMEM),
            pl.BlockSpec(memory_space=pltpu.VMEM),
            pl.BlockSpec(memory_space=pltpu.VMEM),
            pl.BlockSpec(memory_space=pltpu.VMEM),
            pl.BlockSpec(memory_space=pl.ANY),
        ],
        out_specs=pl.BlockSpec(memory_space=pltpu.VMEM),
        scratch_shapes=[
            pltpu.VMEM((XS, 2, SLOTS, PAGE, HEAD_DIM), BF16),
            pltpu.VMEM((XS, 2, rows, HEAD_DIM), BF16),
            pltpu.VMEM((zs, block, HEAD_DIM), BF16),
            pltpu.VMEM((zs, block, HEAD_DIM), BF16),
            pltpu.VMEM((zs, 1, HEAD_DIM), F32),
            pltpu.VMEM((zs, block, HEAD_DIM), BF16),
            pltpu.VMEM((zs, 1, HEAD_DIM), F32),
            pltpu.VMEM((XS * SLOTS, PAGE), F32),
            pltpu.VMEM((block, HEAD_DIM), F32),
            pltpu.VMEM((hs, per, HEAD_DIM), F32),
            dma((XS,)), dma((XS,)), dma((XS,)), dma((XS,)), dma((zs,)), dma((zs,)),
            dma((zs,)), dma((zs,)), dma((zs,)), dma((zs,)), dma((hs,)), dma((hs,)), dma,
        ],
        compiler_params=pltpu.CompilerParams(
            collective_id=0, has_side_effects=True, vmem_limit_bytes=48 * 2**20
        ),
    )(prefix_len, page_slot, queries, new_kv, cache.reshape(2, SLOTS, PAGE, HEAD_DIM))
    result = result.reshape(hs, rows // hs, group * HEAD_DIM)
    return result.transpose(1, 0, 2).reshape(rows // hs, hs * group * HEAD_DIM).astype(BF16)


def solution(mesh):
    zs = mesh.shape["ctx"] // XS
    hs = mesh.shape["head"]
    return jax.shard_map(
        functools.partial(local, zs, hs),
        mesh=mesh,
        in_specs=(P(), P(), P("ctx", "head"), P(None, "ctx", "head"), P(None, "ctx", None, "head")),
        out_specs=P(("ctx", "head"), None),
        check_vma=False,
    )
```

```python
import functools

import jax
import jax.numpy as jnp
from jax import lax
from jax.experimental import pallas as pl
from jax.experimental.pallas import tpu as pltpu
from jax.sharding import PartitionSpec as P

HEAD_DIM = 128
PAGE = 256
SLOTS = 2
XS = 4
ZS = 16
MASKED = -1e30
FLOOR = -1e20
LOG2E = 1.4426950408889634
MESH = pl.DeviceIdType.MESH
F32 = jnp.float32
BF16 = jnp.bfloat16

NEAR = (1, -1, 2, -2)
FAR = 5
UP = (8, 7, 6, 4, 3)
DOWN = (-7, -6, -4, -3)
GROUPS = ((7, 6, 4, 3), (-7, -6, -4, -3), (8, 5, -5, 0), (2, -2, 1, -1))
PARTNERS = (1, -1, 2, -2, 3, -3, 5, -5)


def merge(diagonal, terms):
    top = functools.reduce(jnp.maximum, [stat for _, stat in terms])
    shares = [jnp.exp2(stat - top) for _, stat in terms]
    share_sum = functools.reduce(jnp.add, shares)
    merged = None
    for (values, _), share in zip(terms, shares):
        share = jnp.broadcast_to(share / share_sum, diagonal.shape)
        share = jnp.sum(jnp.where(diagonal, share, 0.0), axis=1, keepdims=True)
        term = share * values.astype(F32)
        merged = term if merged is None else merged + term
    return merged, top + jnp.log2(share_sum)


def kernel(
    hs, rows, group, lens_hbm, slot_hbm, q_hbm, new_hbm, cache_hbm, out_ref,
    lens, table, q_in, kv_all, new_all, q_all, part, part_stat, mid, mid_stat, got, got_stat,
    relay, relay_stat, bias, fin, heads,
    local_sem, kv_send, kv_recv, new_send, new_recv, q_send, q_recv,
    out_send, stat_send, mid_recv, mid_stat_recv, got_recv, got_stat_recv, head_send, head_recv,
):
    ctx = lax.axis_index("ctx")
    head = lax.axis_index("head")
    x, z = ctx // ZS, ctx % ZS
    side = x // (XS // 2)
    block = rows * group
    per = rows // hs * group
    sent = []

    def x_at(k):
        return lax.rem(x + k + XS, XS)

    def z_at(k):
        return lax.rem(z + k + ZS, ZS)

    def at_x(k):
        return (x_at(k) * ZS + z, head)

    def at_z(k):
        return (x * ZS + z_at(k), head)

    def at_head(k):
        return (ctx, lax.rem(head + k, hs))

    def send(src, dst, send_sem, recv_sem, device):
        copy = pltpu.make_async_remote_copy(
            src, dst, send_sem, recv_sem, device_id=device, device_id_type=MESH
        )
        copy.start()
        sent.append(copy)

    def arrived(ref, sem):
        pltpu.make_async_copy(ref, ref, sem).wait()

    loads = [
        pltpu.make_async_copy(q_hbm, q_in, local_sem.at[0]),
        pltpu.make_async_copy(cache_hbm, kv_all.at[0], local_sem.at[1]),
        pltpu.make_async_copy(new_hbm, new_all.at[0], local_sem.at[2]),
        pltpu.make_async_copy(slot_hbm, table, local_sem.at[3]),
        pltpu.make_async_copy(lens_hbm, lens, local_sem.at[4]),
    ]
    for load in loads:
        load.start()

    barrier = pltpu.get_barrier_semaphore()
    partners = [at_x(k) for k in range(1, XS)] + [at_z(k) for k in PARTNERS]
    partners += [at_head(k) for k in range(1, hs)]
    for device in partners:
        pl.semaphore_signal(barrier, inc=1, device_id=device, device_id_type=MESH)

    loads[0].wait()
    queries = q_in[...].astype(F32)
    queries = jnp.concatenate(
        [queries[:, h * HEAD_DIM:(h + 1) * HEAD_DIM] for h in range(group)], axis=0
    )
    q_all[0] = queries.astype(BF16)

    pl.semaphore_wait(barrier, len(partners))

    def send_queries(held, offset):
        there = (held + offset) % ZS
        send(q_all.at[held % ZS], q_all.at[there], q_send.at[there], q_recv.at[there], at_z(offset))

    def send_pages(src, held, slot, offset, number):
        there = (held + offset) % XS
        send(src, kv_all.at[there, :, slot], kv_send.at[number], kv_recv.at[there, slot], at_x(offset))

    for offset in (FAR, -FAR) + NEAR[::-1]:
        send_queries(0, offset)
    send_pages(cache_hbm.at[:, 0], 0, 0, 1, 0)
    send_pages(cache_hbm.at[:, 1], 0, 1, -1, 1)
    send_pages(cache_hbm.at[:, 1], 0, 1, 1, 2)
    send_pages(cache_hbm.at[:, 0], 0, 0, -1, 3)
    for k in range(1, XS):
        send(new_hbm, new_all.at[k], new_send.at[k], new_recv.at[k], at_x(k))

    for load in loads[1:]:
        load.wait()
    pages = table.shape[1]
    page_ids = lax.broadcasted_iota(jnp.int32, (1, pages), 1)
    live = jnp.clip(lens[side] - page_ids * PAGE, 0, PAGE).astype(F32)
    slots = lax.broadcasted_iota(jnp.int32, (XS * SLOTS, pages), 0)
    slots = SLOTS * (lax.rem(x + XS - slots // SLOTS, XS) * ZS + z) + slots % SLOTS
    live = jnp.where(table[pl.ds(side, 1), :] == slots, live, 0.0)
    live = jnp.sum(live, axis=1, keepdims=True)
    offsets = lax.broadcasted_iota(jnp.int32, (XS * SLOTS, PAGE), 1).astype(F32)
    bias[...] = jnp.where(offsets < live, 0.0, MASKED)

    arrived(q_all.at[FAR], q_recv.at[FAR])
    for offset in (3, 2, -2, 1, -1):
        send_queries(FAR, offset)
    arrived(q_all.at[ZS - FAR], q_recv.at[ZS - FAR])
    for offset in (2, -2, 1, -1):
        send_queries(-FAR, offset)
    arrived(kv_all.at[1, :, 0], kv_recv.at[1, 0])
    send_pages(kv_all.at[1, :, 0], 1, 0, 1, 4)
    arrived(kv_all.at[XS - 1, :, 1], kv_recv.at[XS - 1, 1])
    send_pages(kv_all.at[XS - 1, :, 1], -1, 1, -1, 5)

    for d in range(1, ZS):
        if d not in (FAR, ZS - FAR):
            arrived(q_all.at[d], q_recv.at[d])
    for k in range(1, XS):
        arrived(new_all.at[k], new_recv.at[k])
    new_keys = jnp.concatenate([new_all[i, 0].astype(F32) for i in range(XS)], axis=0).astype(BF16)
    new_values = jnp.concatenate([new_all[i, 1].astype(F32) for i in range(XS)], axis=0).astype(BF16)
    fresh = XS * rows
    wide = len(GROUPS[0]) * block
    new_at = lax.broadcasted_iota(jnp.int32, (block, fresh), 1)
    new_rows = rows * (lax.rem(x + XS - new_at // rows, XS) * ZS + z) + new_at % rows
    at = lax.broadcasted_iota(jnp.int32, (block, fresh), 0) % rows
    scale = HEAD_DIM ** (-0.5) * LOG2E
    contract = (((1,), (1,)), ((), ()))
    ones = jnp.ones((SLOTS * PAGE, HEAD_DIM), BF16)
    diagonal = (
        lax.broadcasted_iota(jnp.int32, (block, HEAD_DIM), 0)
        == lax.broadcasted_iota(jnp.int32, (block, HEAD_DIM), 1)
    )
    masks = [
        jnp.concatenate([bias[SLOTS * i + j:SLOTS * i + j + 1, :] for j in range(SLOTS)], axis=1)
        for i in range(XS)
    ]
    for i, slot in ((1, 1), (XS - 1, 0), (2, 0), (2, 1)):
        arrived(kv_all.at[i, :, slot], kv_recv.at[i, slot])

    def attend(members):
        mine = jnp.concatenate([q_all[-d % ZS] for d in members], axis=0)
        scores = []
        for i in range(XS):
            keys = kv_all[i, 0].reshape(SLOTS * PAGE, HEAD_DIM)
            raw = lax.dot_general(mine, keys, contract, preferred_element_type=F32)
            scores.append(raw + masks[i])
        raw = lax.dot_general(mine, new_keys, contract, preferred_element_type=F32)
        seen = [
            (new_rows <= rows * (x * ZS + z_at(d)) + at) & (new_rows >= side * (XS // 2 * ZS * rows))
            for d in members
        ]
        scores.append(raw + jnp.concatenate([jnp.where(s, 0.0, MASKED) for s in seen], axis=0))
        tiles = [
            s[:, j:j + HEAD_DIM] for s in scores[:XS] for j in range(0, SLOTS * PAGE, HEAD_DIM)
        ]
        top = jnp.max(functools.reduce(jnp.maximum, tiles), axis=1, keepdims=True)
        top = jnp.maximum(top, jnp.max(scores[XS], axis=1, keepdims=True))
        top = jnp.maximum(top, FLOOR) * scale
        total = jnp.zeros((wide, 2 * HEAD_DIM), F32)
        for i in range(XS):
            weights = jnp.exp2(scores[i] * scale - top).astype(BF16)
            values = kv_all[i, 1].reshape(SLOTS * PAGE, HEAD_DIM)
            total += jnp.dot(
                weights, jnp.concatenate([values, ones], axis=1), preferred_element_type=F32
            )
        weights = jnp.exp2(scores[XS] * scale - top).astype(BF16)
        total += jnp.dot(
            weights, jnp.concatenate([new_values, ones[:fresh]], axis=1), preferred_element_type=F32
        )
        amount = total[:, HEAD_DIM:]
        full = jnp.maximum(amount, 1.0)
        normal = (total[:, :HEAD_DIM] / full).astype(BF16)
        stat = jnp.where(amount > 0.0, top + jnp.log2(full), MASKED)
        for j, d in enumerate(members):
            part[d % ZS] = normal[j * block:(j + 1) * block]
            part_stat[d % ZS] = jnp.sum(
                jnp.where(diagonal, stat[j * block:(j + 1) * block], 0.0), axis=0, keepdims=True
            )

    def send_part(d, offset, dst, dst_stat, recv, stat_recv, slot):
        number = d % ZS
        send(part.at[number], dst.at[slot], out_send.at[number], recv.at[slot], at_z(offset))
        send(
            part_stat.at[number], dst_stat.at[slot], stat_send.at[number], stat_recv.at[slot],
            at_z(offset),
        )

    mid_slots = {d: i for i, d in enumerate(UP + DOWN)}
    got_slots = {d: i for i, d in enumerate(NEAR + (FAR, -FAR))}
    for members in GROUPS:
        attend(members)
        for d in members:
            if d in mid_slots:
                offset = d - FAR if d > 0 else d + FAR
                send_part(d, offset, mid, mid_stat, mid_recv, mid_stat_recv, mid_slots[d])
            elif d in NEAR:
                send_part(d, d, got, got_stat, got_recv, got_stat_recv, got_slots[d])

    for number, (d, others) in enumerate(((FAR, UP), (-FAR, DOWN))):
        terms = [(part[d % ZS], part_stat[d % ZS])]
        for other in others:
            slot = mid_slots[other]
            arrived(mid.at[slot], mid_recv.at[slot])
            arrived(mid_stat.at[slot], mid_stat_recv.at[slot])
            terms.append((mid[slot], mid_stat[slot]))
        merged, stat = merge(diagonal, terms)
        relay[number] = merged.astype(BF16)
        relay_stat[number] = stat
        slot = got_slots[d]
        send(relay.at[number], got.at[slot], out_send.at[d % ZS], got_recv.at[slot], at_z(d))
        send(
            relay_stat.at[number], got_stat.at[slot], stat_send.at[d % ZS], got_stat_recv.at[slot],
            at_z(d),
        )

    terms = [(part[0], part_stat[0])]
    for slot in got_slots.values():
        arrived(got.at[slot], got_recv.at[slot])
        arrived(got_stat.at[slot], got_stat_recv.at[slot])
        terms.append((got[slot], got_stat[slot]))
    merged, _ = merge(diagonal, terms)
    for h in range(group):
        fin[pl.ds(h, rows, stride=group), :] = merged[h * rows:(h + 1) * rows]

    def fin_at(there):
        return pl.ds(pl.multiple_of(there * per, 8), per)

    for k in range(1, hs):
        there = lax.rem(head + k, hs)
        send(
            fin.at[fin_at(there), :], heads.at[head], head_send.at[k], head_recv.at[head], at_head(k)
        )
    heads[head] = fin[fin_at(head), :]
    for k in range(1, hs):
        there = lax.rem(head + k, hs)
        arrived(heads.at[there], head_recv.at[there])
    out_ref[...] = heads[...]
    for copy in sent:
        copy.wait_send()


def local(hs, prefix_len, page_slot, queries, new_kv, cache):
    rows = queries.shape[0]
    group = queries.shape[1] // HEAD_DIM
    block = rows * group
    per = rows // hs * group
    mids = len(UP + DOWN)
    gots = len(NEAR) + 2
    dma = pltpu.SemaphoreType.DMA
    result = pl.pallas_call(
        functools.partial(kernel, hs, rows, group),
        out_shape=jax.ShapeDtypeStruct((hs, per, HEAD_DIM), F32),
        in_specs=[pl.BlockSpec(memory_space=pltpu.HBM)] * 5,
        out_specs=pl.BlockSpec(memory_space=pltpu.VMEM),
        scratch_shapes=[
            pltpu.SMEM(prefix_len.shape, jnp.int32),
            pltpu.VMEM(page_slot.shape, jnp.int32),
            pltpu.VMEM(queries.shape, BF16),
            pltpu.VMEM((XS, 2, SLOTS, PAGE, HEAD_DIM), BF16),
            pltpu.VMEM((XS, 2, rows, HEAD_DIM), BF16),
            pltpu.VMEM((ZS, block, HEAD_DIM), BF16),
            pltpu.VMEM((ZS, block, HEAD_DIM), BF16),
            pltpu.VMEM((ZS, 1, HEAD_DIM), F32),
            pltpu.VMEM((mids, block, HEAD_DIM), BF16),
            pltpu.VMEM((mids, 1, HEAD_DIM), F32),
            pltpu.VMEM((gots, block, HEAD_DIM), BF16),
            pltpu.VMEM((gots, 1, HEAD_DIM), F32),
            pltpu.VMEM((2, block, HEAD_DIM), BF16),
            pltpu.VMEM((2, 1, HEAD_DIM), F32),
            pltpu.VMEM((XS * SLOTS, PAGE), F32),
            pltpu.VMEM((block, HEAD_DIM), F32),
            pltpu.VMEM((hs, per, HEAD_DIM), F32),
            dma((5,)), dma((6,)), dma((XS, SLOTS)), dma((XS,)), dma((XS,)), dma((ZS,)), dma((ZS,)),
            dma((ZS,)), dma((ZS,)), dma((mids,)), dma((mids,)), dma((gots,)), dma((gots,)),
            dma((hs,)), dma((hs,)),
        ],
        compiler_params=pltpu.CompilerParams(
            collective_id=0, has_side_effects=True, vmem_limit_bytes=62 * 2**20
        ),
    )(prefix_len, page_slot, queries, new_kv, cache.reshape(2, SLOTS, PAGE, HEAD_DIM))
    result = result.reshape(hs, rows // hs, group * HEAD_DIM)
    return result.transpose(1, 0, 2).reshape(rows // hs, hs * group * HEAD_DIM).astype(BF16)


def solution(mesh):
    return jax.shard_map(
        functools.partial(local, mesh.shape["head"]),
        mesh=mesh,
        in_specs=(P(), P(), P("ctx", "head"), P(None, "ctx", "head"), P(None, "ctx", None, "head")),
        out_specs=P(("ctx", "head"), None),
        check_vma=False,
    )
```

```python
import functools

import jax
import jax.numpy as jnp
from jax import lax
from jax.experimental import pallas as pl
from jax.experimental.pallas import tpu as pltpu
from jax.sharding import PartitionSpec as P

HEAD_DIM = 128
PAGE = 256
SLOTS = 2
XS = 4
ZS = 16
MASKED = -1e30
FLOOR = -1e20
LOG2E = 1.4426950408889634
MESH = pl.DeviceIdType.MESH
F32 = jnp.float32
BF16 = jnp.bfloat16

NEAR = (2, -2, 1, -1)
FAR = 5
HALF = 8
RELAY = HALF - FAR
SETS = {t: (t, t - FAR, t + FAR) for t in NEAR}
ORDER = sum(SETS.values(), ()) + (-FAR, FAR, 0, HALF)
FIRST = (NEAR, (0, -FAR, FAR), (-3, 7, -7, 3, HALF), (-4, 6, -6, 4))
SECOND = (FIRST[2], FIRST[3], FIRST[1], FIRST[0])
PARTNERS = (1, -1, 2, -2, RELAY, -RELAY, FAR, -FAR)


def merge(diagonal, terms):
    top = functools.reduce(jnp.maximum, [stat for _, stat in terms])
    shares = [jnp.exp2(stat - top) for _, stat in terms]
    share_sum = functools.reduce(jnp.add, shares)
    merged = None
    for (values, _), share in zip(terms, shares):
        share = jnp.broadcast_to(share / share_sum, diagonal.shape)
        share = jnp.sum(jnp.where(diagonal, share, 0.0), axis=1, keepdims=True)
        term = share * values.astype(F32)
        merged = term if merged is None else merged + term
    return merged, top + jnp.log2(share_sum)


def kernel(
    hs, rows, group, lens_hbm, slot_hbm, q_hbm, new_hbm, cache_hbm, out_ref,
    lens, table, q_in, kv_all, new_all, q_all, part, part_stat, box, box_stat, pair, pair_stat,
    half, half_stat, final, final_stat, last, last_stat, tops, totals, bias, wide, heads,
    local_sem, kv_send, kv_recv, new_send, new_recv, q_send, q_recv, out_send, stat_send,
    pair_send, pair_stat_send, box_recv, box_stat_recv, pair_recv, pair_stat_recv, half_recv,
    last_send, last_stat_send, last_recv, last_stat_recv,
):
    ctx = lax.axis_index("ctx")
    head = lax.axis_index("head")
    x, z = ctx // ZS, ctx % ZS
    side = x // (XS // 2)
    block = rows * group
    own = rows // hs
    sent = []
    at_slot = {d: i for i, d in enumerate(ORDER)}

    def z_at(k):
        return lax.rem(z + k + ZS, ZS)

    def at_x(k):
        return (lax.rem(x + k + XS, XS) * ZS + z, head)

    def at_z(k):
        return (x * ZS + z_at(k), head)

    def at_head(k):
        return (ctx, lax.rem(head + k, hs))

    def send(src, dst, send_sem, recv_sem, device):
        copy = pltpu.make_async_remote_copy(
            src, dst, send_sem, recv_sem, device_id=device, device_id_type=MESH
        )
        copy.start()
        sent.append(copy)

    def arrived(ref, sem):
        pltpu.make_async_copy(ref, ref, sem).wait()

    barrier = pltpu.get_barrier_semaphore()
    partners = [at_x(k) for k in range(1, XS)] + [at_z(k) for k in PARTNERS]
    partners += [at_head(k) for k in range(1, hs)]
    for device in partners:
        pl.semaphore_signal(barrier, inc=1, device_id=device, device_id_type=MESH)

    loads = [
        pltpu.make_async_copy(q_hbm, q_in, local_sem.at[0]),
        pltpu.make_async_copy(cache_hbm, kv_all.at[0], local_sem.at[1]),
        pltpu.make_async_copy(new_hbm, new_all.at[0], local_sem.at[2]),
        pltpu.make_async_copy(slot_hbm, table, local_sem.at[3]),
        pltpu.make_async_copy(lens_hbm, lens, local_sem.at[4]),
    ]
    for load in loads:
        load.start()

    pl.semaphore_wait(barrier, len(partners))

    def send_pages(src, held, slot, offset, number):
        there = (held + offset) % XS
        send(src, kv_all.at[there, :, slot], kv_send.at[number], kv_recv.at[there, slot], at_x(offset))

    send_pages(cache_hbm.at[:, 0], 0, 0, 1, 0)
    send_pages(cache_hbm.at[:, 1], 0, 1, -1, 1)
    send_pages(cache_hbm.at[:, 1], 0, 1, 1, 2)
    send_pages(cache_hbm.at[:, 0], 0, 0, -1, 3)

    def slot_of(d, count=1):
        return pl.ds(at_slot[d], count)

    def send_queries(src, dst, count, offset):
        dst = slot_of(dst, count)
        number = at_slot[offset] if count == 1 else at_slot[offset] + 1
        recv = at_slot[-offset] if count == 1 else at_slot[-offset] + 1
        send(q_all.at[slot_of(src, count)], q_all.at[dst], q_send.at[number], q_recv.at[recv], at_z(offset))

    def queries_arrived(d, count=1):
        arrived(q_all.at[slot_of(d, count)], q_recv.at[at_slot[d]])

    loads[0].wait()
    queries = q_in[...].astype(F32)
    for h in range(group):
        wide[pl.ds(h, rows, stride=group), :] = queries[:, h * HEAD_DIM:(h + 1) * HEAD_DIM]
    q_all[at_slot[0]] = wide[...].astype(BF16)
    for offset in (FAR, -FAR) + NEAR:
        send_queries(0, -offset, 1, offset)
    for k in range(1, XS):
        send(new_hbm, new_all.at[k], new_send.at[k], new_recv.at[k], at_x(k))

    for load in loads[1:]:
        load.wait()
    pages = table.shape[1]
    page_ids = lax.broadcasted_iota(jnp.int32, (1, pages), 1)
    live = jnp.clip(lens[side] - page_ids * PAGE, 0, PAGE).astype(F32)
    slots = lax.broadcasted_iota(jnp.int32, (XS * SLOTS, pages), 0)
    slots = SLOTS * (lax.rem(x + XS - slots // SLOTS, XS) * ZS + z) + slots % SLOTS
    live = jnp.where(table[pl.ds(side, 1), :] == slots, live, 0.0)
    live = jnp.sum(live, axis=1, keepdims=True)
    offsets = lax.broadcasted_iota(jnp.int32, (XS * SLOTS, PAGE), 1).astype(F32)
    bias[...] = jnp.where(offsets < live, 0.0, MASKED)

    arrived(kv_all.at[1, :, 0], kv_recv.at[1, 0])
    send_pages(kv_all.at[1, :, 0], 1, 0, 1, 4)
    arrived(kv_all.at[XS - 1, :, 1], kv_recv.at[XS - 1, 1])
    send_pages(kv_all.at[XS - 1, :, 1], -1, 1, -1, 5)
    queries_arrived(-FAR)
    send(
        q_all.at[slot_of(-FAR)], q_all.at[slot_of(HALF)], q_send.at[at_slot[HALF]],
        q_recv.at[at_slot[HALF]], at_z(RELAY),
    )
    queries_arrived(FAR)
    for offset in NEAR:
        send_queries(-FAR, SETS[-offset][1], 2, offset)

    for k in range(1, XS):
        arrived(new_all.at[k], new_recv.at[k])
    new_keys = jnp.concatenate([new_all[i, 0].astype(F32) for i in range(XS)], axis=0).astype(BF16)
    new_values = jnp.concatenate([new_all[i, 1].astype(F32) for i in range(XS)], axis=0).astype(BF16)
    fresh = XS * rows
    new_at = lax.broadcasted_iota(jnp.int32, (block, fresh), 1)
    new_rows = rows * (lax.rem(x + XS - new_at // rows, XS) * ZS + z) + new_at % rows
    at = lax.broadcasted_iota(jnp.int32, (block, fresh), 0) // group
    scale = HEAD_DIM ** (-0.5) * LOG2E
    contract = (((1,), (1,)), ((), ()))
    ones = jnp.ones((SLOTS * PAGE, HEAD_DIM), BF16)
    diagonal = (
        lax.broadcasted_iota(jnp.int32, (block, HEAD_DIM), 0)
        == lax.broadcasted_iota(jnp.int32, (block, HEAD_DIM), 1)
    )

    def gathered(members):
        return jnp.concatenate([q_all[at_slot[d]] for d in members], axis=0)

    def score(mine, i):
        keys = kv_all[i, 0].reshape(SLOTS * PAGE, HEAD_DIM)
        raw = lax.dot_general(mine, keys, contract, preferred_element_type=F32)
        return raw + jnp.concatenate(
            [bias[SLOTS * i + j:SLOTS * i + j + 1, :] for j in range(SLOTS)], axis=1
        )

    def highest(scores):
        tiles = [s[:, j:j + HEAD_DIM] for s in scores for j in range(0, SLOTS * PAGE, HEAD_DIM)]
        return jnp.max(functools.reduce(jnp.maximum, tiles), axis=1, keepdims=True)

    def weigh(scores, top, i):
        weights = jnp.exp2(scores * scale - top).astype(BF16)
        values = kv_all[i, 1].reshape(SLOTS * PAGE, HEAD_DIM)
        return jnp.dot(
            weights, jnp.concatenate([values, ones], axis=1), preferred_element_type=F32
        )

    def attend_first(members):
        mine = gathered(members)
        here = (0, 1, XS - 1)
        scores = [score(mine, i) for i in here]
        raw = lax.dot_general(mine, new_keys, contract, preferred_element_type=F32)
        seen = [
            (new_rows <= rows * (x * ZS + z_at(d)) + at) & (new_rows >= side * (XS // 2 * ZS * rows))
            for d in members
        ]
        new_scores = raw + jnp.concatenate([jnp.where(s, 0.0, MASKED) for s in seen], axis=0)
        top = jnp.maximum(highest(scores), jnp.max(new_scores, axis=1, keepdims=True))
        top = jnp.maximum(top, FLOOR) * scale
        weights = jnp.exp2(new_scores * scale - top).astype(BF16)
        total = jnp.dot(
            weights, jnp.concatenate([new_values, ones[:fresh]], axis=1), preferred_element_type=F32
        )
        for i, s in zip(here, scores):
            total += weigh(s, top, i)
        top = jnp.broadcast_to(top, (top.shape[0], HEAD_DIM))
        for j, d in enumerate(members):
            tops[at_slot[d]] = top[j * block:(j + 1) * block]
            totals[at_slot[d]] = total[j * block:(j + 1) * block]

    def attend_second(members):
        scores = score(gathered(members), 2)
        before = jnp.concatenate([tops[at_slot[d]] for d in members], axis=0)
        total = jnp.concatenate([totals[at_slot[d]] for d in members], axis=0)
        top = jnp.maximum(before, highest([scores]) * scale)
        fade = jnp.exp2(before - top)
        total = total * jnp.concatenate([fade, fade], axis=1)
        total += weigh(scores, top[:, :1], 2)
        amount = total[:, HEAD_DIM:]
        full = jnp.maximum(amount, 1.0)
        normal = (total[:, :HEAD_DIM] / full).astype(BF16)
        stat = jnp.where(amount > 0.0, top + jnp.log2(full), MASKED)
        for j, d in enumerate(members):
            part[at_slot[d]] = normal[j * block:(j + 1) * block]
            part_stat[at_slot[d]] = jnp.sum(
                jnp.where(diagonal, stat[j * block:(j + 1) * block], 0.0), axis=0, keepdims=True
            )

    arrived(kv_all.at[1, :, 1], kv_recv.at[1, 1])
    arrived(kv_all.at[XS - 1, :, 0], kv_recv.at[XS - 1, 0])
    for t in NEAR:
        queries_arrived(t)
    attend_first(FIRST[0])
    attend_first(FIRST[1])
    queries_arrived(HALF)
    for t in NEAR:
        queries_arrived(SETS[t][1], 2)
    attend_first(FIRST[2])
    attend_first(FIRST[3])
    for slot in range(SLOTS):
        arrived(kv_all.at[2, :, slot], kv_recv.at[2, slot])

    def send_parts(d, count, dst, dst_stat, data_sems, stat_sems, offset):
        send(part.at[slot_of(d, count)], dst, *data_sems, at_z(offset))
        send(part_stat.at[slot_of(d, count)], dst_stat, *stat_sems, at_z(offset))

    def send_pair(t):
        here, there = NEAR.index(t), NEAR.index(-t)
        send_parts(
            SETS[t][1], 2, pair.at[there], pair_stat.at[there],
            (pair_send.at[here], pair_recv.at[there]),
            (pair_stat_send.at[here], pair_stat_recv.at[there]), t,
        )

    def send_near(t):
        here, there = NEAR.index(t), NEAR.index(-t)
        send_parts(
            t, 1, box.at[pl.ds(there, 1)], box_stat.at[pl.ds(there, 1)],
            (out_send.at[here], box_recv.at[there]), (stat_send.at[here], box_stat_recv.at[there]), t,
        )

    attend_second(SECOND[0])
    send_parts(
        HALF, 1, half, half_stat, (out_send.at[4], half_recv.at[0]),
        (stat_send.at[4], half_recv.at[1]), RELAY,
    )
    send_pair(2)
    send_pair(-2)
    attend_second(SECOND[1])
    send_pair(1)
    send_pair(-1)
    attend_second(SECOND[2])
    attend_second(SECOND[3])
    for t in NEAR:
        send_near(t)

    def send_final(number, offset, k):
        there = lax.rem(head + k, hs)
        device = (x * ZS + z_at(offset), there)
        send(
            final.at[number, pl.ds(there * own, own)], last.at[number, head],
            last_send.at[number, k], last_recv.at[number, head], device,
        )
        send(
            final_stat.at[number], last_stat.at[number, head],
            last_stat_send.at[number, k], last_stat_recv.at[number, head], device,
        )

    for i in range(len(NEAR)):
        arrived(pair.at[i], pair_recv.at[i])
        arrived(pair_stat.at[i], pair_stat_recv.at[i])
    for number, d in enumerate((-FAR, FAR)):
        terms = [(part[at_slot[d]], part_stat[at_slot[d]])]
        terms += [(pair[i, number], pair_stat[i, number]) for i in range(len(NEAR))]
        if d == FAR:
            arrived(half, half_recv.at[0])
            arrived(half_stat, half_recv.at[1])
            terms.append((half[0], half_stat[0]))
        merged, stat = merge(diagonal, terms)
        final[1 + number] = merged.astype(BF16).reshape(rows, group, HEAD_DIM)
        final_stat[1 + number] = stat
        for k in range(hs):
            send_final(1 + number, d, k)
    terms = [(part[at_slot[0]], part_stat[at_slot[0]])]
    for i in range(len(NEAR)):
        arrived(box.at[i], box_recv.at[i])
        arrived(box_stat.at[i], box_stat_recv.at[i])
        terms.append((box[i], box_stat[i]))
    merged, stat = merge(diagonal, terms)
    final[0] = merged.astype(BF16).reshape(rows, group, HEAD_DIM)
    final_stat[0] = stat
    for k in range(1, hs):
        send_final(0, 0, k)
    last[0, head] = final[0, pl.ds(head * own, own)]
    last_stat[0, head] = stat
    for copy in sent:
        copy.wait_send()
    for number in range(3):
        for k in range(0 if number else 1, hs):
            there = lax.rem(head + k, hs)
            arrived(last.at[number, there], last_recv.at[number, there])
            arrived(last_stat.at[number, there], last_stat_recv.at[number, there])
    mine = (own * group, HEAD_DIM)
    diagonal = (
        lax.broadcasted_iota(jnp.int32, mine, 0) + head * own * group
        == lax.broadcasted_iota(jnp.int32, mine, 1)
    )
    for g in range(hs):
        terms = [(last[number, g].reshape(mine), last_stat[number, g]) for number in range(3)]
        heads[g] = merge(diagonal, terms)[0]
    for i in range(own):
        pieces = [heads[g, i * group + h:i * group + h + 1, :] for g in range(hs) for h in range(group)]
        out_ref[i:i + 1, :] = jnp.concatenate(pieces, axis=1).astype(BF16)


def local(hs, prefix_len, page_slot, queries, new_kv, cache):
    rows = queries.shape[0]
    group = queries.shape[1] // HEAD_DIM
    block = rows * group
    own = rows // hs
    near = len(NEAR)
    dma = pltpu.SemaphoreType.DMA
    return pl.pallas_call(
        functools.partial(kernel, hs, rows, group),
        out_shape=jax.ShapeDtypeStruct((rows // hs, hs * group * HEAD_DIM), BF16),
        in_specs=[pl.BlockSpec(memory_space=pltpu.HBM)] * 5,
        out_specs=pl.BlockSpec(memory_space=pltpu.VMEM),
        scratch_shapes=[
            pltpu.SMEM(prefix_len.shape, jnp.int32),
            pltpu.VMEM(page_slot.shape, jnp.int32),
            pltpu.VMEM(queries.shape, BF16),
            pltpu.VMEM((XS, 2, SLOTS, PAGE, HEAD_DIM), BF16),
            pltpu.VMEM((XS, 2, rows, HEAD_DIM), BF16),
            pltpu.VMEM((ZS, block, HEAD_DIM), BF16),
            pltpu.VMEM((ZS, block, HEAD_DIM), BF16),
            pltpu.VMEM((ZS, 1, HEAD_DIM), F32),
            pltpu.VMEM((near, block, HEAD_DIM), BF16),
            pltpu.VMEM((near, 1, HEAD_DIM), F32),
            pltpu.VMEM((near, 2, block, HEAD_DIM), BF16),
            pltpu.VMEM((near, 2, 1, HEAD_DIM), F32),
            pltpu.VMEM((1, block, HEAD_DIM), BF16),
            pltpu.VMEM((1, 1, HEAD_DIM), F32),
            pltpu.VMEM((3, rows, group, HEAD_DIM), BF16),
            pltpu.VMEM((3, 1, HEAD_DIM), F32),
            pltpu.VMEM((3, hs, own, group, HEAD_DIM), BF16),
            pltpu.VMEM((3, hs, 1, HEAD_DIM), F32),
            pltpu.VMEM((ZS, block, HEAD_DIM), F32),
            pltpu.VMEM((ZS, block, 2 * HEAD_DIM), F32),
            pltpu.VMEM((XS * SLOTS, PAGE), F32),
            pltpu.VMEM((block, HEAD_DIM), F32),
            pltpu.VMEM((hs, own * group, HEAD_DIM), F32),
            dma((5,)), dma((6,)), dma((XS, SLOTS)), dma((XS,)), dma((XS,)), dma((ZS,)), dma((ZS,)),
            dma((near + 1,)), dma((near + 1,)), dma((near,)), dma((near,)), dma((near,)),
            dma((near,)), dma((near,)), dma((near,)), dma((2,)),
            dma((3, hs)), dma((3, hs)), dma((3, hs)), dma((3, hs)),
        ],
        compiler_params=pltpu.CompilerParams(
            collective_id=0, has_side_effects=True, vmem_limit_bytes=62 * 2**20
        ),
    )(prefix_len, page_slot, queries, new_kv, cache.reshape(2, SLOTS, PAGE, HEAD_DIM))


def solution(mesh):
    return jax.shard_map(
        functools.partial(local, mesh.shape["head"]),
        mesh=mesh,
        in_specs=(P(), P(), P("ctx", "head"), P(None, "ctx", "head"), P(None, "ctx", None, "head")),
        out_specs=P(("ctx", "head"), None),
        check_vma=False,
    )
```

```python
import functools

import jax
import jax.numpy as jnp
from jax import lax
from jax.experimental import pallas as pl
from jax.experimental.pallas import tpu as pltpu
from jax.sharding import PartitionSpec as P

HEAD_DIM = 128
PAGE = 256
SLOTS = 2
XS = 4
ZS = 16
MASKED = -1e30
FLOOR = -1e20
LOG2E = 1.4426950408889634
MESH = pl.DeviceIdType.MESH
F32 = jnp.float32
BF16 = jnp.bfloat16

NEAR = (2, -2, 1, -1)
FAR = 5
HALF = 8
RELAY = HALF - FAR
SETS = {t: (t, t - FAR, t + FAR) for t in NEAR}
ORDER = sum(SETS.values(), ()) + (-FAR, FAR, 0, HALF)
FIRST = (NEAR, (0, -FAR, FAR), (-3, 7, -7, 3, HALF), (-4, 6, -6, 4))
SECOND = (FIRST[2], FIRST[3], FIRST[1], FIRST[0])
PARTNERS = (1, -1, 2, -2, RELAY, -RELAY, FAR, -FAR)


def merge(diagonal, terms):
    top = functools.reduce(jnp.maximum, [stat for _, stat in terms])
    shares = [jnp.exp2(stat - top) for _, stat in terms]
    share_sum = functools.reduce(jnp.add, shares)
    merged = None
    for (values, _), share in zip(terms, shares):
        share = jnp.broadcast_to(share / share_sum, diagonal.shape)
        share = jnp.sum(jnp.where(diagonal, share, 0.0), axis=1, keepdims=True)
        term = share * values.astype(F32)
        merged = term if merged is None else merged + term
    return merged, top + jnp.log2(share_sum)


def kernel(
    hs, rows, group, lens_hbm, slot_hbm, q_hbm, new_hbm, cache_hbm, out_ref,
    lens, table, q_in, kv_all, new_all, q_all, part, part_stat, box, box_stat, pair, pair_stat,
    half, half_stat, final, final_stat, last, last_stat, tops, totals, bias, wide, heads,
    local_sem, kv_send, kv_recv, new_send, new_recv, q_send, q_recv, out_send, stat_send,
    pair_send, pair_stat_send, box_recv, box_stat_recv, pair_recv, pair_stat_recv, half_recv,
    last_send, last_stat_send, last_recv, last_stat_recv,
):
    ctx = lax.axis_index("ctx")
    head = lax.axis_index("head")
    x, z = ctx // ZS, ctx % ZS
    side = x // (XS // 2)
    block = rows * group
    own = rows // hs
    sent = []
    at_slot = {d: i for i, d in enumerate(ORDER)}

    def z_at(k):
        return lax.rem(z + k + ZS, ZS)

    def at_x(k):
        return (lax.rem(x + k + XS, XS) * ZS + z, head)

    def at_z(k):
        return (x * ZS + z_at(k), head)

    def at_head(k):
        return (ctx, lax.rem(head + k, hs))

    def send(src, dst, send_sem, recv_sem, device):
        copy = pltpu.make_async_remote_copy(
            src, dst, send_sem, recv_sem, device_id=device, device_id_type=MESH
        )
        copy.start()
        sent.append(copy)

    def arrived(ref, sem):
        pltpu.make_async_copy(ref, ref, sem).wait()

    barrier = pltpu.get_barrier_semaphore()
    partners = [at_x(k) for k in range(1, XS)] + [at_z(k) for k in PARTNERS]
    partners += [at_head(k) for k in range(1, hs)]
    for device in partners:
        pl.semaphore_signal(barrier, inc=1, device_id=device, device_id_type=MESH)

    loads = [
        pltpu.make_async_copy(q_hbm, q_in, local_sem.at[0]),
        pltpu.make_async_copy(cache_hbm, kv_all.at[0], local_sem.at[1]),
        pltpu.make_async_copy(new_hbm, new_all.at[0], local_sem.at[2]),
        pltpu.make_async_copy(slot_hbm, table, local_sem.at[3]),
        pltpu.make_async_copy(lens_hbm, lens, local_sem.at[4]),
    ]
    for load in loads:
        load.start()

    pl.semaphore_wait(barrier, len(partners))

    def send_pages(src, held, slot, offset, number):
        there = (held + offset) % XS
        send(src, kv_all.at[there, :, slot], kv_send.at[number], kv_recv.at[there, slot], at_x(offset))

    send_pages(cache_hbm.at[:, 0], 0, 0, 1, 0)
    send_pages(cache_hbm.at[:, 1], 0, 1, -1, 1)
    send_pages(cache_hbm.at[:, 1], 0, 1, 1, 2)
    send_pages(cache_hbm.at[:, 0], 0, 0, -1, 3)

    def slot_of(d, count=1):
        return pl.ds(at_slot[d], count)

    def send_queries(src, dst, count, offset):
        dst = slot_of(dst, count)
        number = at_slot[offset] if count == 1 else at_slot[offset] + 1
        recv = at_slot[-offset] if count == 1 else at_slot[-offset] + 1
        send(q_all.at[slot_of(src, count)], q_all.at[dst], q_send.at[number], q_recv.at[recv], at_z(offset))

    def queries_arrived(d, count=1):
        arrived(q_all.at[slot_of(d, count)], q_recv.at[at_slot[d]])

    loads[0].wait()
    queries = q_in[...].astype(F32)
    for h in range(group):
        wide[pl.ds(h, rows, stride=group), :] = queries[:, h * HEAD_DIM:(h + 1) * HEAD_DIM]
    q_all[at_slot[0]] = wide[...].astype(BF16)
    for offset in (FAR, -FAR) + NEAR:
        send_queries(0, -offset, 1, offset)
    for k in range(1, XS):
        send(new_hbm, new_all.at[k], new_send.at[k], new_recv.at[k], at_x(k))

    for load in loads[1:]:
        load.wait()
    pages = table.shape[1]
    page_ids = lax.broadcasted_iota(jnp.int32, (1, pages), 1)
    live = jnp.clip(lens[side] - page_ids * PAGE, 0, PAGE).astype(F32)
    slots = lax.broadcasted_iota(jnp.int32, (XS * SLOTS, pages), 0)
    slots = SLOTS * (lax.rem(x + XS - slots // SLOTS, XS) * ZS + z) + slots % SLOTS
    live = jnp.where(table[pl.ds(side, 1), :] == slots, live, 0.0)
    live = jnp.sum(live, axis=1, keepdims=True)
    offsets = lax.broadcasted_iota(jnp.int32, (XS * SLOTS, PAGE), 1).astype(F32)
    bias[...] = jnp.where(offsets < live, 0.0, MASKED)

    arrived(kv_all.at[1, :, 0], kv_recv.at[1, 0])
    send_pages(kv_all.at[1, :, 0], 1, 0, 1, 4)
    arrived(kv_all.at[XS - 1, :, 1], kv_recv.at[XS - 1, 1])
    send_pages(kv_all.at[XS - 1, :, 1], -1, 1, -1, 5)
    queries_arrived(-FAR)
    send(
        q_all.at[slot_of(-FAR)], q_all.at[slot_of(HALF)], q_send.at[at_slot[HALF]],
        q_recv.at[at_slot[HALF]], at_z(RELAY),
    )
    queries_arrived(FAR)
    for offset in NEAR:
        send_queries(-FAR, SETS[-offset][1], 2, offset)

    for k in range(1, XS):
        arrived(new_all.at[k], new_recv.at[k])
    new_keys = jnp.concatenate([new_all[i, 0].astype(F32) for i in range(XS)], axis=0).astype(BF16)
    new_values = jnp.concatenate([new_all[i, 1].astype(F32) for i in range(XS)], axis=0).astype(BF16)
    fresh = XS * rows
    new_at = lax.broadcasted_iota(jnp.int32, (block, fresh), 1)
    new_rows = rows * (lax.rem(x + XS - new_at // rows, XS) * ZS + z) + new_at % rows
    at = lax.broadcasted_iota(jnp.int32, (block, fresh), 0) // group
    scale = HEAD_DIM ** (-0.5) * LOG2E
    contract = (((1,), (1,)), ((), ()))
    ones = jnp.ones((SLOTS * PAGE, HEAD_DIM), BF16)
    diagonal = (
        lax.broadcasted_iota(jnp.int32, (block, HEAD_DIM), 0)
        == lax.broadcasted_iota(jnp.int32, (block, HEAD_DIM), 1)
    )

    def gathered(members):
        return jnp.concatenate([q_all[at_slot[d]] for d in members], axis=0)

    def score(mine, i):
        keys = kv_all[i, 0].reshape(SLOTS * PAGE, HEAD_DIM)
        raw = lax.dot_general(mine, keys, contract, preferred_element_type=F32)
        return raw + jnp.concatenate(
            [bias[SLOTS * i + j:SLOTS * i + j + 1, :] for j in range(SLOTS)], axis=1
        )

    def highest(scores):
        tiles = [s[:, j:j + HEAD_DIM] for s in scores for j in range(0, SLOTS * PAGE, HEAD_DIM)]
        return jnp.max(functools.reduce(jnp.maximum, tiles), axis=1, keepdims=True)

    def weigh(scores, top, i):
        weights = jnp.exp2(scores * scale - top).astype(BF16)
        values = kv_all[i, 1].reshape(SLOTS * PAGE, HEAD_DIM)
        return jnp.dot(
            weights, jnp.concatenate([values, ones], axis=1), preferred_element_type=F32
        )

    def attend_first(members):
        mine = gathered(members)
        here = (0, 1, XS - 1)
        scores = [score(mine, i) for i in here]
        raw = lax.dot_general(mine, new_keys, contract, preferred_element_type=F32)
        seen = [
            (new_rows <= rows * (x * ZS + z_at(d)) + at) & (new_rows >= side * (XS // 2 * ZS * rows))
            for d in members
        ]
        new_scores = raw + jnp.concatenate([jnp.where(s, 0.0, MASKED) for s in seen], axis=0)
        top = jnp.maximum(highest(scores), jnp.max(new_scores, axis=1, keepdims=True))
        top = jnp.maximum(top, FLOOR) * scale
        weights = jnp.exp2(new_scores * scale - top).astype(BF16)
        total = jnp.dot(
            weights, jnp.concatenate([new_values, ones[:fresh]], axis=1), preferred_element_type=F32
        )
        for i, s in zip(here, scores):
            total += weigh(s, top, i)
        top = jnp.broadcast_to(top, (top.shape[0], HEAD_DIM))
        for j, d in enumerate(members):
            tops[at_slot[d]] = top[j * block:(j + 1) * block]
            totals[at_slot[d]] = total[j * block:(j + 1) * block]

    def attend_second(members):
        scores = score(gathered(members), 2)
        before = jnp.concatenate([tops[at_slot[d]] for d in members], axis=0)
        total = jnp.concatenate([totals[at_slot[d]] for d in members], axis=0)
        top = jnp.maximum(before, highest([scores]) * scale)
        fade = jnp.exp2(before - top)
        total = total * jnp.concatenate([fade, fade], axis=1)
        total += weigh(scores, top[:, :1], 2)
        amount = total[:, HEAD_DIM:]
        full = jnp.maximum(amount, 1.0)
        normal = (total[:, :HEAD_DIM] / full).astype(BF16)
        stat = jnp.where(amount > 0.0, top + jnp.log2(full), MASKED)
        for j, d in enumerate(members):
            part[at_slot[d]] = normal[j * block:(j + 1) * block]
            part_stat[at_slot[d]] = jnp.sum(
                jnp.where(diagonal, stat[j * block:(j + 1) * block], 0.0), axis=0, keepdims=True
            )

    arrived(kv_all.at[1, :, 1], kv_recv.at[1, 1])
    arrived(kv_all.at[XS - 1, :, 0], kv_recv.at[XS - 1, 0])
    for t in NEAR:
        queries_arrived(t)
    attend_first(FIRST[0])
    attend_first(FIRST[1])
    queries_arrived(HALF)
    for t in NEAR:
        queries_arrived(SETS[t][1], 2)
    attend_first(FIRST[2])
    attend_first(FIRST[3])
    for slot in range(SLOTS):
        arrived(kv_all.at[2, :, slot], kv_recv.at[2, slot])

    def send_parts(d, count, dst, dst_stat, data_sems, stat_sems, offset):
        send(part.at[slot_of(d, count)], dst, *data_sems, at_z(offset))
        send(part_stat.at[slot_of(d, count)], dst_stat, *stat_sems, at_z(offset))

    def send_pair(t):
        here, there = NEAR.index(t), NEAR.index(-t)
        send_parts(
            SETS[t][1], 2, pair.at[there], pair_stat.at[there],
            (pair_send.at[here], pair_recv.at[there]),
            (pair_stat_send.at[here], pair_stat_recv.at[there]), t,
        )

    def send_near(t):
        here, there = NEAR.index(t), NEAR.index(-t)
        send_parts(
            t, 1, box.at[pl.ds(there, 1)], box_stat.at[pl.ds(there, 1)],
            (out_send.at[here], box_recv.at[there]), (stat_send.at[here], box_stat_recv.at[there]), t,
        )

    attend_second(SECOND[0])
    send_parts(
        HALF, 1, half, half_stat, (out_send.at[4], half_recv.at[0]),
        (stat_send.at[4], half_recv.at[1]), RELAY,
    )
    send_pair(2)
    send_pair(-2)
    attend_second(SECOND[1])
    send_pair(1)
    send_pair(-1)
    attend_second(SECOND[2])
    attend_second(SECOND[3])
    for t in NEAR:
        send_near(t)

    def send_final(number, offset, k):
        there = lax.rem(head + k, hs)
        device = (x * ZS + z_at(offset), there)
        send(
            final.at[number, pl.ds(there * own, own)], last.at[number, head],
            last_send.at[number, k], last_recv.at[number, head], device,
        )
        send(
            final_stat.at[number], last_stat.at[number, head],
            last_stat_send.at[number, k], last_stat_recv.at[number, head], device,
        )

    for i in range(len(NEAR)):
        arrived(pair.at[i], pair_recv.at[i])
        arrived(pair_stat.at[i], pair_stat_recv.at[i])
    for number, d in enumerate((-FAR, FAR)):
        terms = [(part[at_slot[d]], part_stat[at_slot[d]])]
        terms += [(pair[i, number], pair_stat[i, number]) for i in range(len(NEAR))]
        if d == FAR:
            arrived(half, half_recv.at[0])
            arrived(half_stat, half_recv.at[1])
            terms.append((half[0], half_stat[0]))
        merged, stat = merge(diagonal, terms)
        final[1 + number] = merged.astype(BF16).reshape(rows, group, HEAD_DIM)
        final_stat[1 + number] = stat
        for k in range(hs):
            send_final(1 + number, d, k)
    terms = [(part[at_slot[0]], part_stat[at_slot[0]])]
    for i in range(len(NEAR)):
        arrived(box.at[i], box_recv.at[i])
        arrived(box_stat.at[i], box_stat_recv.at[i])
        terms.append((box[i], box_stat[i]))
    merged, stat = merge(diagonal, terms)
    final[0] = merged.astype(BF16).reshape(rows, group, HEAD_DIM)
    final_stat[0] = stat
    for k in range(1, hs):
        send_final(0, 0, k)
    last[0, head] = final[0, pl.ds(head * own, own)]
    last_stat[0, head] = stat
    for copy in sent:
        copy.wait_send()
    for number in range(3):
        for k in range(0 if number else 1, hs):
            there = lax.rem(head + k, hs)
            arrived(last.at[number, there], last_recv.at[number, there])
            arrived(last_stat.at[number, there], last_stat_recv.at[number, there])
    mine = (own * group, HEAD_DIM)
    diagonal = (
        lax.broadcasted_iota(jnp.int32, mine, 0) + head * own * group
        == lax.broadcasted_iota(jnp.int32, mine, 1)
    )
    for g in range(hs):
        terms = [(last[number, g].reshape(mine), last_stat[number, g]) for number in range(3)]
        heads[g] = merge(diagonal, terms)[0]
    for i in range(own):
        pieces = [heads[g, i * group + h:i * group + h + 1, :] for g in range(hs) for h in range(group)]
        out_ref[i:i + 1, :] = jnp.concatenate(pieces, axis=1).astype(BF16)


def local(hs, prefix_len, page_slot, queries, new_kv, cache):
    rows = queries.shape[0]
    group = queries.shape[1] // HEAD_DIM
    block = rows * group
    own = rows // hs
    near = len(NEAR)
    dma = pltpu.SemaphoreType.DMA
    return pl.pallas_call(
        functools.partial(kernel, hs, rows, group),
        out_shape=jax.ShapeDtypeStruct((rows // hs, hs * group * HEAD_DIM), BF16),
        in_specs=[pl.BlockSpec(memory_space=pltpu.HBM)] * 5,
        out_specs=pl.BlockSpec(memory_space=pltpu.VMEM),
        scratch_shapes=[
            pltpu.SMEM(prefix_len.shape, jnp.int32),
            pltpu.VMEM(page_slot.shape, jnp.int32),
            pltpu.VMEM(queries.shape, BF16),
            pltpu.VMEM((XS, 2, SLOTS, PAGE, HEAD_DIM), BF16),
            pltpu.VMEM((XS, 2, rows, HEAD_DIM), BF16),
            pltpu.VMEM((ZS, block, HEAD_DIM), BF16),
            pltpu.VMEM((ZS, block, HEAD_DIM), BF16),
            pltpu.VMEM((ZS, 1, HEAD_DIM), F32),
            pltpu.VMEM((near, block, HEAD_DIM), BF16),
            pltpu.VMEM((near, 1, HEAD_DIM), F32),
            pltpu.VMEM((near, 2, block, HEAD_DIM), BF16),
            pltpu.VMEM((near, 2, 1, HEAD_DIM), F32),
            pltpu.VMEM((1, block, HEAD_DIM), BF16),
            pltpu.VMEM((1, 1, HEAD_DIM), F32),
            pltpu.VMEM((3, rows, group, HEAD_DIM), BF16),
            pltpu.VMEM((3, 1, HEAD_DIM), F32),
            pltpu.VMEM((3, hs, own, group, HEAD_DIM), BF16),
            pltpu.VMEM((3, hs, 1, HEAD_DIM), F32),
            pltpu.VMEM((ZS, block, HEAD_DIM), F32),
            pltpu.VMEM((ZS, block, 2 * HEAD_DIM), F32),
            pltpu.VMEM((XS * SLOTS, PAGE), F32),
            pltpu.VMEM((block, HEAD_DIM), F32),
            pltpu.VMEM((hs, own * group, HEAD_DIM), F32),
            dma((5,)), dma((6,)), dma((XS, SLOTS)), dma((XS,)), dma((XS,)), dma((ZS,)), dma((ZS,)),
            dma((near + 1,)), dma((near + 1,)), dma((near,)), dma((near,)), dma((near,)),
            dma((near,)), dma((near,)), dma((near,)), dma((2,)),
            dma((3, hs)), dma((3, hs)), dma((3, hs)), dma((3, hs)),
        ],
        compiler_params=pltpu.CompilerParams(
            collective_id=0, has_side_effects=True, vmem_limit_bytes=48 * 2**20
        ),
    )(*[pltpu.with_memory_space_constraint(a, pltpu.HBM) for a in (prefix_len, page_slot, queries, new_kv, cache.reshape(2, SLOTS, PAGE, HEAD_DIM))])


def solution(mesh):
    return jax.shard_map(
        functools.partial(local, mesh.shape["head"]),
        mesh=mesh,
        in_specs=(P(), P(), P("ctx", "head"), P(None, "ctx", "head"), P(None, "ctx", None, "head")),
        out_specs=P(("ctx", "head"), None),
        check_vma=False,
    )
```

```python
import functools

import jax
import jax.numpy as jnp
from jax import lax
from jax.experimental import pallas as pl
from jax.experimental.pallas import tpu as pltpu
from jax.sharding import PartitionSpec as P

HEAD_DIM = 128
PAGE = 256
SLOTS = 2
XS = 4
ZS = 16
MASKED = -1e30
FLOOR = -1e20
LOG2E = 1.4426950408889634
MESH = pl.DeviceIdType.MESH
F32 = jnp.float32
BF16 = jnp.bfloat16

NEAR = (2, -2, 1, -1)
FAR = 5
HALF = 8
RELAY = HALF - FAR
SETS = {t: (t, t - FAR, t + FAR) for t in NEAR}
ORDER = sum(SETS.values(), ()) + (-FAR, FAR, 0, HALF)
FIRST = (NEAR, (0, -FAR, FAR), (-3, 7, -7, 3, HALF), (-4, 6, -6, 4))
SECOND = (FIRST[2], FIRST[3], FIRST[1], FIRST[0])
PARTNERS = (1, -1, 2, -2, RELAY, -RELAY, FAR, -FAR)


def merge(diagonal, terms):
    top = functools.reduce(jnp.maximum, [stat for _, stat in terms])
    shares = [jnp.exp2(stat - top) for _, stat in terms]
    share_sum = functools.reduce(jnp.add, shares)
    merged = None
    for (values, _), share in zip(terms, shares):
        share = jnp.broadcast_to(share / share_sum, diagonal.shape)
        share = jnp.sum(jnp.where(diagonal, share, 0.0), axis=1, keepdims=True)
        term = share * values.astype(F32)
        merged = term if merged is None else merged + term
    return merged, top + jnp.log2(share_sum)


def kernel(
    hs, rows, group, lens_hbm, slot_hbm, q_hbm, new_hbm, cache_hbm, out_ref,
    lens, table, q_in, kv_all, new_all, q_all, part, part_stat, box, box_stat, pair, pair_stat,
    half, half_stat, final, final_stat, last, last_stat, tops, totals, bias, wide, heads,
    local_sem, kv_send, kv_recv, new_send, new_recv, q_send, q_recv, out_send, stat_send,
    pair_send, pair_stat_send, box_recv, box_stat_recv, pair_recv, pair_stat_recv, half_recv,
    last_send, last_stat_send, last_recv, last_stat_recv,
):
    ctx = lax.axis_index("ctx")
    head = lax.axis_index("head")
    x, z = ctx // ZS, ctx % ZS
    side = x // (XS // 2)
    block = rows * group
    own = rows // hs
    sent = []
    at_slot = {d: i for i, d in enumerate(ORDER)}

    def z_at(k):
        return lax.rem(z + k + ZS, ZS)

    def at_x(k):
        return (lax.rem(x + k + XS, XS) * ZS + z, head)

    def at_z(k):
        return (x * ZS + z_at(k), head)

    def at_head(k):
        return (ctx, lax.rem(head + k, hs))

    def send(src, dst, send_sem, recv_sem, device):
        copy = pltpu.make_async_remote_copy(
            src, dst, send_sem, recv_sem, device_id=device, device_id_type=MESH
        )
        copy.start()
        sent.append(copy)

    def arrived(ref, sem):
        pltpu.make_async_copy(ref, ref, sem).wait()

    barrier = pltpu.get_barrier_semaphore()
    partners = [at_z(k) for k in PARTNERS] + [at_head(k) for k in range(1, hs)]
    partners += [at_x(k) for k in range(1, XS)]
    for device in partners:
        pl.semaphore_signal(barrier, inc=1, device_id=device, device_id_type=MESH)

    loads = [
        pltpu.make_async_copy(q_hbm, q_in, local_sem.at[0]),
        pltpu.make_async_copy(cache_hbm, kv_all.at[0], local_sem.at[1]),
        pltpu.make_async_copy(new_hbm, new_all.at[0], local_sem.at[2]),
        pltpu.make_async_copy(slot_hbm, table, local_sem.at[3]),
        pltpu.make_async_copy(lens_hbm, lens, local_sem.at[4]),
    ]
    for load in loads:
        load.start()

    loads[0].wait()
    queries = q_in[...].astype(F32)
    for h in range(group):
        wide[pl.ds(h, rows, stride=group), :] = queries[:, h * HEAD_DIM:(h + 1) * HEAD_DIM]
    q_all[at_slot[0]] = wide[...].astype(BF16)
    for load in loads[1:]:
        load.wait()
    pages = table.shape[1]
    page_ids = lax.broadcasted_iota(jnp.int32, (1, pages), 1)
    live = jnp.clip(lens[side] - page_ids * PAGE, 0, PAGE).astype(F32)
    slots = lax.broadcasted_iota(jnp.int32, (XS * SLOTS, pages), 0)
    slots = SLOTS * (lax.rem(x + XS - slots // SLOTS, XS) * ZS + z) + slots % SLOTS
    live = jnp.where(table[pl.ds(side, 1), :] == slots, live, 0.0)
    live = jnp.sum(live, axis=1, keepdims=True)
    offsets = lax.broadcasted_iota(jnp.int32, (XS * SLOTS, PAGE), 1).astype(F32)
    bias[...] = jnp.where(offsets < live, 0.0, MASKED)

    pl.semaphore_wait(barrier, len(partners))

    def send_pages(src, held, slot, offset, number):
        there = (held + offset) % XS
        send(src, kv_all.at[there, :, slot], kv_send.at[number], kv_recv.at[there, slot], at_x(offset))

    send_pages(cache_hbm.at[:, 0], 0, 0, 1, 0)
    send_pages(cache_hbm.at[:, 1], 0, 1, -1, 1)
    send_pages(cache_hbm.at[:, 1], 0, 1, 1, 2)
    send_pages(cache_hbm.at[:, 0], 0, 0, -1, 3)

    def slot_of(d, count=1):
        return pl.ds(at_slot[d], count)

    def send_queries(src, dst, count, offset):
        dst = slot_of(dst, count)
        number = at_slot[offset] if count == 1 else at_slot[offset] + 1
        recv = at_slot[-offset] if count == 1 else at_slot[-offset] + 1
        send(q_all.at[slot_of(src, count)], q_all.at[dst], q_send.at[number], q_recv.at[recv], at_z(offset))

    def queries_arrived(d, count=1):
        arrived(q_all.at[slot_of(d, count)], q_recv.at[at_slot[d]])

    for offset in (FAR, -FAR) + NEAR:
        send_queries(0, -offset, 1, offset)
    for k in range(1, XS):
        send(new_hbm, new_all.at[k], new_send.at[k], new_recv.at[k], at_x(k))

    queries_arrived(-FAR)
    send(
        q_all.at[slot_of(-FAR)], q_all.at[slot_of(HALF)], q_send.at[at_slot[HALF]],
        q_recv.at[at_slot[HALF]], at_z(RELAY),
    )
    queries_arrived(FAR)
    for offset in NEAR:
        send_queries(-FAR, SETS[-offset][1], 2, offset)

    arrived(kv_all.at[1, :, 0], kv_recv.at[1, 0])
    send_pages(kv_all.at[1, :, 0], 1, 0, 1, 4)
    arrived(kv_all.at[XS - 1, :, 1], kv_recv.at[XS - 1, 1])
    send_pages(kv_all.at[XS - 1, :, 1], -1, 1, -1, 5)
    for k in range(1, XS):
        arrived(new_all.at[k], new_recv.at[k])
    new_keys = jnp.concatenate([new_all[i, 0].astype(F32) for i in range(XS)], axis=0).astype(BF16)
    new_values = jnp.concatenate([new_all[i, 1].astype(F32) for i in range(XS)], axis=0).astype(BF16)
    fresh = XS * rows
    new_at = lax.broadcasted_iota(jnp.int32, (block, fresh), 1)
    new_rows = rows * (lax.rem(x + XS - new_at // rows, XS) * ZS + z) + new_at % rows
    at = lax.broadcasted_iota(jnp.int32, (block, fresh), 0) // group
    scale = HEAD_DIM ** (-0.5) * LOG2E
    contract = (((1,), (1,)), ((), ()))
    ones = jnp.ones((SLOTS * PAGE, HEAD_DIM), BF16)
    diagonal = (
        lax.broadcasted_iota(jnp.int32, (block, HEAD_DIM), 0)
        == lax.broadcasted_iota(jnp.int32, (block, HEAD_DIM), 1)
    )

    def gathered(members):
        return jnp.concatenate([q_all[at_slot[d]] for d in members], axis=0)

    def score(mine, i):
        keys = kv_all[i, 0].reshape(SLOTS * PAGE, HEAD_DIM)
        raw = lax.dot_general(mine, keys, contract, preferred_element_type=F32)
        return raw + jnp.concatenate(
            [bias[SLOTS * i + j:SLOTS * i + j + 1, :] for j in range(SLOTS)], axis=1
        )

    def highest(scores):
        tiles = [s[:, j:j + HEAD_DIM] for s in scores for j in range(0, SLOTS * PAGE, HEAD_DIM)]
        return jnp.max(functools.reduce(jnp.maximum, tiles), axis=1, keepdims=True)

    def weigh(scores, top, i):
        weights = jnp.exp2(scores * scale - top).astype(BF16)
        values = kv_all[i, 1].reshape(SLOTS * PAGE, HEAD_DIM)
        return jnp.dot(
            weights, jnp.concatenate([values, ones], axis=1), preferred_element_type=F32
        )

    def attend_first(members, here=(0, 1, XS - 1)):
        mine = gathered(members)
        scores = [score(mine, i) for i in here]
        raw = lax.dot_general(mine, new_keys, contract, preferred_element_type=F32)
        seen = [
            (new_rows <= rows * (x * ZS + z_at(d)) + at) & (new_rows >= side * (XS // 2 * ZS * rows))
            for d in members
        ]
        new_scores = raw + jnp.concatenate([jnp.where(s, 0.0, MASKED) for s in seen], axis=0)
        top = jnp.maximum(highest(scores), jnp.max(new_scores, axis=1, keepdims=True))
        top = jnp.maximum(top, FLOOR) * scale
        weights = jnp.exp2(new_scores * scale - top).astype(BF16)
        total = jnp.dot(
            weights, jnp.concatenate([new_values, ones[:fresh]], axis=1), preferred_element_type=F32
        )
        for i, s in zip(here, scores):
            total += weigh(s, top, i)
        top = jnp.broadcast_to(top, (top.shape[0], HEAD_DIM))
        if len(here) == XS:
            finish(members, top, total)
            return
        for j, d in enumerate(members):
            tops[at_slot[d]] = top[j * block:(j + 1) * block]
            totals[at_slot[d]] = total[j * block:(j + 1) * block]

    def attend_second(members):
        scores = score(gathered(members), 2)
        before = jnp.concatenate([tops[at_slot[d]] for d in members], axis=0)
        total = jnp.concatenate([totals[at_slot[d]] for d in members], axis=0)
        top = jnp.maximum(before, highest([scores]) * scale)
        fade = jnp.exp2(before - top)
        total = total * jnp.concatenate([fade, fade], axis=1)
        total += weigh(scores, top[:, :1], 2)
        finish(members, top, total)

    def finish(members, top, total):
        amount = total[:, HEAD_DIM:]
        full = jnp.maximum(amount, 1.0)
        normal = (total[:, :HEAD_DIM] / full).astype(BF16)
        stat = jnp.where(amount > 0.0, top + jnp.log2(full), MASKED)
        for j, d in enumerate(members):
            part[at_slot[d]] = normal[j * block:(j + 1) * block]
            part_stat[at_slot[d]] = jnp.sum(
                jnp.where(diagonal, stat[j * block:(j + 1) * block], 0.0), axis=0, keepdims=True
            )

    arrived(kv_all.at[1, :, 1], kv_recv.at[1, 1])
    arrived(kv_all.at[XS - 1, :, 0], kv_recv.at[XS - 1, 0])
    queries_arrived(HALF)
    for t in NEAR:
        queries_arrived(SETS[t][1], 2)
    attend_first(FIRST[2])
    attend_first(FIRST[3])
    for t in NEAR:
        queries_arrived(t)
    for slot in range(SLOTS):
        arrived(kv_all.at[2, :, slot], kv_recv.at[2, slot])

    def send_parts(d, count, dst, dst_stat, data_sems, stat_sems, offset):
        send(part.at[slot_of(d, count)], dst, *data_sems, at_z(offset))
        send(part_stat.at[slot_of(d, count)], dst_stat, *stat_sems, at_z(offset))

    def send_pair(t):
        here, there = NEAR.index(t), NEAR.index(-t)
        send_parts(
            SETS[t][1], 2, pair.at[there], pair_stat.at[there],
            (pair_send.at[here], pair_recv.at[there]),
            (pair_stat_send.at[here], pair_stat_recv.at[there]), t,
        )

    def send_near(t):
        here, there = NEAR.index(t), NEAR.index(-t)
        send_parts(
            t, 1, box.at[pl.ds(there, 1)], box_stat.at[pl.ds(there, 1)],
            (out_send.at[here], box_recv.at[there]), (stat_send.at[here], box_stat_recv.at[there]), t,
        )

    attend_second(SECOND[0])
    send_parts(
        HALF, 1, half, half_stat, (out_send.at[4], half_recv.at[0]),
        (stat_send.at[4], half_recv.at[1]), RELAY,
    )
    send_pair(2)
    send_pair(-2)
    attend_second(SECOND[1])
    send_pair(1)
    send_pair(-1)
    attend_first(FIRST[1], range(XS))
    attend_first(FIRST[0], range(XS))
    for t in NEAR:
        send_near(t)

    def send_final(number, offset, k):
        there = lax.rem(head + k, hs)
        device = (x * ZS + z_at(offset), there)
        send(
            final.at[number, pl.ds(there * own, own)], last.at[number, head],
            last_send.at[number, k], last_recv.at[number, head], device,
        )
        send(
            final_stat.at[number], last_stat.at[number, head],
            last_stat_send.at[number, k], last_stat_recv.at[number, head], device,
        )

    for i in range(len(NEAR)):
        arrived(pair.at[i], pair_recv.at[i])
        arrived(pair_stat.at[i], pair_stat_recv.at[i])
    for number, d in enumerate((-FAR, FAR)):
        terms = [(part[at_slot[d]], part_stat[at_slot[d]])]
        terms += [(pair[i, number], pair_stat[i, number]) for i in range(len(NEAR))]
        if d == FAR:
            arrived(half, half_recv.at[0])
            arrived(half_stat, half_recv.at[1])
            terms.append((half[0], half_stat[0]))
        merged, stat = merge(diagonal, terms)
        final[1 + number] = merged.astype(BF16).reshape(rows, group, HEAD_DIM)
        final_stat[1 + number] = stat
        for k in range(hs):
            send_final(1 + number, d, k)
    terms = [(part[at_slot[0]], part_stat[at_slot[0]])]
    for i in range(len(NEAR)):
        arrived(box.at[i], box_recv.at[i])
        arrived(box_stat.at[i], box_stat_recv.at[i])
        terms.append((box[i], box_stat[i]))
    merged, stat = merge(diagonal, terms)
    final[0] = merged.astype(BF16).reshape(rows, group, HEAD_DIM)
    final_stat[0] = stat
    for k in range(1, hs):
        send_final(0, 0, k)
    last[0, head] = final[0, pl.ds(head * own, own)]
    last_stat[0, head] = stat
    for copy in sent:
        copy.wait_send()
    for number in range(3):
        for k in range(0 if number else 1, hs):
            there = lax.rem(head + k, hs)
            arrived(last.at[number, there], last_recv.at[number, there])
            arrived(last_stat.at[number, there], last_stat_recv.at[number, there])
    mine = (own * group, HEAD_DIM)
    diagonal = (
        lax.broadcasted_iota(jnp.int32, mine, 0) + head * own * group
        == lax.broadcasted_iota(jnp.int32, mine, 1)
    )
    for g in range(hs):
        terms = [(last[number, g].reshape(mine), last_stat[number, g]) for number in range(3)]
        heads[g] = merge(diagonal, terms)[0]
    for i in range(own):
        pieces = [heads[g, i * group + h:i * group + h + 1, :] for g in range(hs) for h in range(group)]
        out_ref[i:i + 1, :] = jnp.concatenate(pieces, axis=1).astype(BF16)


def local(hs, prefix_len, page_slot, queries, new_kv, cache):
    rows = queries.shape[0]
    group = queries.shape[1] // HEAD_DIM
    block = rows * group
    own = rows // hs
    near = len(NEAR)
    dma = pltpu.SemaphoreType.DMA
    return pl.pallas_call(
        functools.partial(kernel, hs, rows, group),
        out_shape=jax.ShapeDtypeStruct((rows // hs, hs * group * HEAD_DIM), BF16),
        in_specs=[pl.BlockSpec(memory_space=pltpu.HBM)] * 5,
        out_specs=pl.BlockSpec(memory_space=pltpu.VMEM),
        scratch_shapes=[
            pltpu.SMEM(prefix_len.shape, jnp.int32),
            pltpu.VMEM(page_slot.shape, jnp.int32),
            pltpu.VMEM(queries.shape, BF16),
            pltpu.VMEM((XS, 2, SLOTS, PAGE, HEAD_DIM), BF16),
            pltpu.VMEM((XS, 2, rows, HEAD_DIM), BF16),
            pltpu.VMEM((ZS, block, HEAD_DIM), BF16),
            pltpu.VMEM((ZS, block, HEAD_DIM), BF16),
            pltpu.VMEM((ZS, 1, HEAD_DIM), F32),
            pltpu.VMEM((near, block, HEAD_DIM), BF16),
            pltpu.VMEM((near, 1, HEAD_DIM), F32),
            pltpu.VMEM((near, 2, block, HEAD_DIM), BF16),
            pltpu.VMEM((near, 2, 1, HEAD_DIM), F32),
            pltpu.VMEM((1, block, HEAD_DIM), BF16),
            pltpu.VMEM((1, 1, HEAD_DIM), F32),
            pltpu.VMEM((3, rows, group, HEAD_DIM), BF16),
            pltpu.VMEM((3, 1, HEAD_DIM), F32),
            pltpu.VMEM((3, hs, own, group, HEAD_DIM), BF16),
            pltpu.VMEM((3, hs, 1, HEAD_DIM), F32),
            pltpu.VMEM((ZS, block, HEAD_DIM), F32),
            pltpu.VMEM((ZS, block, 2 * HEAD_DIM), F32),
            pltpu.VMEM((XS * SLOTS, PAGE), F32),
            pltpu.VMEM((block, HEAD_DIM), F32),
            pltpu.VMEM((hs, own * group, HEAD_DIM), F32),
            dma((5,)), dma((6,)), dma((XS, SLOTS)), dma((XS,)), dma((XS,)), dma((ZS,)), dma((ZS,)),
            dma((near + 1,)), dma((near + 1,)), dma((near,)), dma((near,)), dma((near,)),
            dma((near,)), dma((near,)), dma((near,)), dma((2,)),
            dma((3, hs)), dma((3, hs)), dma((3, hs)), dma((3, hs)),
        ],
        compiler_params=pltpu.CompilerParams(
            collective_id=0, has_side_effects=True, vmem_limit_bytes=48 * 2**20
        ),
    )(*[pltpu.with_memory_space_constraint(a, pltpu.HBM) for a in (prefix_len, page_slot, queries, new_kv, cache.reshape(2, SLOTS, PAGE, HEAD_DIM))])


def solution(mesh):
    return jax.shard_map(
        functools.partial(local, mesh.shape["head"]),
        mesh=mesh,
        in_specs=(P(), P(), P("ctx", "head"), P(None, "ctx", "head"), P(None, "ctx", None, "head")),
        out_specs=P(("ctx", "head"), None),
        check_vma=False,
    )
```

```python
import functools

import jax
import jax.numpy as jnp
from jax import lax
from jax.experimental import pallas as pl
from jax.experimental.pallas import tpu as pltpu
from jax.sharding import PartitionSpec as P

HEAD_DIM = 128
PAGE = 256
SLOTS = 2
XS = 4
ZS = 16
MASKED = -1e30
FLOOR = -1e20
LOG2E = 1.4426950408889634
MESH = pl.DeviceIdType.MESH
F32 = jnp.float32
BF16 = jnp.bfloat16

NEAR = (2, -2, 1, -1)
FAR = 5
HALF = 8
RELAY = HALF - FAR
SETS = {t: (t, t - FAR, t + FAR) for t in NEAR}
ORDER = sum(SETS.values(), ()) + (-FAR, FAR, 0, HALF)
FIRST = (NEAR, (0, -FAR, FAR), (-3, 7, -7, 3, HALF), (-4, 6, -6, 4))
SECOND = (FIRST[2], FIRST[3], FIRST[1], FIRST[0])
PARTNERS = (FAR, -FAR, RELAY, -RELAY, 2, -2, 1, -1)


def merge(diagonal, terms):
    top = functools.reduce(jnp.maximum, [stat for _, stat in terms])
    shares = [jnp.exp2(stat - top) for _, stat in terms]
    share_sum = functools.reduce(jnp.add, shares)
    merged = None
    for (values, _), share in zip(terms, shares):
        share = jnp.broadcast_to(share / share_sum, diagonal.shape)
        share = jnp.sum(jnp.where(diagonal, share, 0.0), axis=1, keepdims=True)
        term = share * values.astype(F32)
        merged = term if merged is None else merged + term
    return merged, top + jnp.log2(share_sum)


def kernel(
    hs, rows, group, lens_hbm, slot_hbm, q_hbm, new_hbm, cache_hbm, out_ref,
    lens, table, q_in, kv_all, new_all, q_all, part, part_stat, box, box_stat, pair, pair_stat,
    half, half_stat, final, final_stat, last, last_stat, tops, totals, bias, wide, heads,
    local_sem, kv_send, kv_recv, new_send, new_recv, q_send, q_recv, out_send, stat_send,
    pair_send, pair_stat_send, box_recv, box_stat_recv, pair_recv, pair_stat_recv, half_recv,
    last_send, last_stat_send, last_recv, last_stat_recv,
):
    ctx = lax.axis_index("ctx")
    head = lax.axis_index("head")
    x, z = ctx // ZS, ctx % ZS
    side = x // (XS // 2)
    block = rows * group
    own = rows // hs
    sent = []
    at_slot = {d: i for i, d in enumerate(ORDER)}

    def z_at(k):
        return lax.rem(z + k + ZS, ZS)

    def at_x(k):
        return (lax.rem(x + k + XS, XS) * ZS + z, head)

    def at_z(k):
        return (x * ZS + z_at(k), head)

    def at_head(k):
        return (ctx, lax.rem(head + k, hs))

    def send(src, dst, send_sem, recv_sem, device):
        copy = pltpu.make_async_remote_copy(
            src, dst, send_sem, recv_sem, device_id=device, device_id_type=MESH
        )
        copy.start()
        sent.append(copy)

    def arrived(ref, sem):
        pltpu.make_async_copy(ref, ref, sem).wait()

    barrier = pltpu.get_barrier_semaphore()
    partners = [at_z(k) for k in PARTNERS] + [at_head(k) for k in range(1, hs)]
    partners += [at_x(k) for k in range(1, XS)]
    for device in partners:
        pl.semaphore_signal(barrier, inc=1, device_id=device, device_id_type=MESH)

    loads = [
        pltpu.make_async_copy(q_hbm, q_in, local_sem.at[0]),
        pltpu.make_async_copy(cache_hbm, kv_all.at[0], local_sem.at[1]),
        pltpu.make_async_copy(new_hbm, new_all.at[0], local_sem.at[2]),
        pltpu.make_async_copy(slot_hbm, table, local_sem.at[3]),
        pltpu.make_async_copy(lens_hbm, lens, local_sem.at[4]),
    ]
    for load in loads:
        load.start()

    loads[0].wait()
    queries = q_in[...].astype(F32)
    for h in range(group):
        wide[pl.ds(h, rows, stride=group), :] = queries[:, h * HEAD_DIM:(h + 1) * HEAD_DIM]
    q_all[at_slot[0]] = wide[...].astype(BF16)
    for load in loads[1:]:
        load.wait()
    pages = table.shape[1]
    page_ids = lax.broadcasted_iota(jnp.int32, (1, pages), 1)
    live = jnp.clip(lens[side] - page_ids * PAGE, 0, PAGE).astype(F32)
    slots = lax.broadcasted_iota(jnp.int32, (XS * SLOTS, pages), 0)
    slots = SLOTS * (lax.rem(x + XS - slots // SLOTS, XS) * ZS + z) + slots % SLOTS
    live = jnp.where(table[pl.ds(side, 1), :] == slots, live, 0.0)
    live = jnp.sum(live, axis=1, keepdims=True)
    offsets = lax.broadcasted_iota(jnp.int32, (XS * SLOTS, PAGE), 1).astype(F32)
    bias[...] = jnp.where(offsets < live, 0.0, MASKED)

    pl.semaphore_wait(barrier, len(partners))

    def send_pages(src, held, slot, offset, number):
        there = (held + offset) % XS
        send(src, kv_all.at[there, :, slot], kv_send.at[number], kv_recv.at[there, slot], at_x(offset))

    send_pages(cache_hbm.at[:, 0], 0, 0, 1, 0)
    send_pages(cache_hbm.at[:, 1], 0, 1, -1, 1)
    send_pages(cache_hbm.at[:, 1], 0, 1, 1, 2)
    send_pages(cache_hbm.at[:, 0], 0, 0, -1, 3)

    def slot_of(d, count=1):
        return pl.ds(at_slot[d], count)

    def send_queries(src, dst, count, offset):
        dst = slot_of(dst, count)
        number = at_slot[offset] if count == 1 else at_slot[offset] + 1
        recv = at_slot[-offset] if count == 1 else at_slot[-offset] + 1
        send(q_all.at[slot_of(src, count)], q_all.at[dst], q_send.at[number], q_recv.at[recv], at_z(offset))

    def queries_arrived(d, count=1):
        arrived(q_all.at[slot_of(d, count)], q_recv.at[at_slot[d]])

    for offset in (FAR, -FAR) + NEAR:
        send_queries(0, -offset, 1, offset)
    for k in range(1, XS):
        send(new_hbm, new_all.at[k], new_send.at[k], new_recv.at[k], at_x(k))

    queries_arrived(-FAR)
    send(
        q_all.at[slot_of(-FAR)], q_all.at[slot_of(HALF)], q_send.at[at_slot[HALF]],
        q_recv.at[at_slot[HALF]], at_z(RELAY),
    )
    queries_arrived(FAR)
    for offset in NEAR:
        send_queries(-FAR, SETS[-offset][1], 2, offset)

    arrived(kv_all.at[1, :, 0], kv_recv.at[1, 0])
    send_pages(kv_all.at[1, :, 0], 1, 0, 1, 4)
    arrived(kv_all.at[XS - 1, :, 1], kv_recv.at[XS - 1, 1])
    send_pages(kv_all.at[XS - 1, :, 1], -1, 1, -1, 5)
    for k in range(1, XS):
        arrived(new_all.at[k], new_recv.at[k])
    new_keys = jnp.concatenate([new_all[i, 0].astype(F32) for i in range(XS)], axis=0).astype(BF16)
    new_values = jnp.concatenate([new_all[i, 1].astype(F32) for i in range(XS)], axis=0).astype(BF16)
    fresh = XS * rows
    new_at = lax.broadcasted_iota(jnp.int32, (block, fresh), 1)
    new_rows = rows * (lax.rem(x + XS - new_at // rows, XS) * ZS + z) + new_at % rows
    at = lax.broadcasted_iota(jnp.int32, (block, fresh), 0) // group
    scale = HEAD_DIM ** (-0.5) * LOG2E
    contract = (((1,), (1,)), ((), ()))
    ones = jnp.ones((SLOTS * PAGE, HEAD_DIM), BF16)
    diagonal = (
        lax.broadcasted_iota(jnp.int32, (block, HEAD_DIM), 0)
        == lax.broadcasted_iota(jnp.int32, (block, HEAD_DIM), 1)
    )

    def gathered(members):
        return jnp.concatenate([q_all[at_slot[d]] for d in members], axis=0)

    def score(mine, i):
        keys = kv_all[i, 0].reshape(SLOTS * PAGE, HEAD_DIM)
        raw = lax.dot_general(mine, keys, contract, preferred_element_type=F32)
        return raw + jnp.concatenate(
            [bias[SLOTS * i + j:SLOTS * i + j + 1, :] for j in range(SLOTS)], axis=1
        )

    def highest(scores):
        tiles = [s[:, j:j + HEAD_DIM] for s in scores for j in range(0, SLOTS * PAGE, HEAD_DIM)]
        return jnp.max(functools.reduce(jnp.maximum, tiles), axis=1, keepdims=True)

    def weigh(scores, top, i):
        weights = jnp.exp2(scores * scale - top).astype(BF16)
        values = kv_all[i, 1].reshape(SLOTS * PAGE, HEAD_DIM)
        return jnp.dot(
            weights, jnp.concatenate([values, ones], axis=1), preferred_element_type=F32
        )

    def attend_first(members, here=(0, 1, XS - 1)):
        mine = gathered(members)
        scores = [score(mine, i) for i in here]
        raw = lax.dot_general(mine, new_keys, contract, preferred_element_type=F32)
        seen = [
            (new_rows <= rows * (x * ZS + z_at(d)) + at) & (new_rows >= side * (XS // 2 * ZS * rows))
            for d in members
        ]
        new_scores = raw + jnp.concatenate([jnp.where(s, 0.0, MASKED) for s in seen], axis=0)
        top = jnp.maximum(highest(scores), jnp.max(new_scores, axis=1, keepdims=True))
        top = jnp.maximum(top, FLOOR) * scale
        weights = jnp.exp2(new_scores * scale - top).astype(BF16)
        total = jnp.dot(
            weights, jnp.concatenate([new_values, ones[:fresh]], axis=1), preferred_element_type=F32
        )
        for i, s in zip(here, scores):
            total += weigh(s, top, i)
        top = jnp.broadcast_to(top, (top.shape[0], HEAD_DIM))
        if len(here) == XS:
            finish(members, top, total)
            return
        for j, d in enumerate(members):
            tops[at_slot[d]] = top[j * block:(j + 1) * block]
            totals[at_slot[d]] = total[j * block:(j + 1) * block]

    def attend_second(members):
        scores = score(gathered(members), 2)
        before = jnp.concatenate([tops[at_slot[d]] for d in members], axis=0)
        total = jnp.concatenate([totals[at_slot[d]] for d in members], axis=0)
        top = jnp.maximum(before, highest([scores]) * scale)
        fade = jnp.exp2(before - top)
        total = total * jnp.concatenate([fade, fade], axis=1)
        total += weigh(scores, top[:, :1], 2)
        finish(members, top, total)

    def finish(members, top, total):
        amount = total[:, HEAD_DIM:]
        full = jnp.maximum(amount, 1.0)
        normal = (total[:, :HEAD_DIM] / full).astype(BF16)
        stat = jnp.where(amount > 0.0, top + jnp.log2(full), MASKED)
        for j, d in enumerate(members):
            part[at_slot[d]] = normal[j * block:(j + 1) * block]
            part_stat[at_slot[d]] = jnp.sum(
                jnp.where(diagonal, stat[j * block:(j + 1) * block], 0.0), axis=0, keepdims=True
            )

    arrived(kv_all.at[1, :, 1], kv_recv.at[1, 1])
    arrived(kv_all.at[XS - 1, :, 0], kv_recv.at[XS - 1, 0])
    queries_arrived(HALF)
    for t in NEAR:
        queries_arrived(SETS[t][1], 2)
    attend_first(FIRST[2])
    attend_first(FIRST[3])
    for t in NEAR:
        queries_arrived(t)
    for slot in range(SLOTS):
        arrived(kv_all.at[2, :, slot], kv_recv.at[2, slot])

    def send_parts(d, count, dst, dst_stat, data_sems, stat_sems, offset):
        send(part.at[slot_of(d, count)], dst, *data_sems, at_z(offset))
        send(part_stat.at[slot_of(d, count)], dst_stat, *stat_sems, at_z(offset))

    def send_pair(t):
        here, there = NEAR.index(t), NEAR.index(-t)
        send_parts(
            SETS[t][1], 2, pair.at[there], pair_stat.at[there],
            (pair_send.at[here], pair_recv.at[there]),
            (pair_stat_send.at[here], pair_stat_recv.at[there]), t,
        )

    def send_near(t):
        here, there = NEAR.index(t), NEAR.index(-t)
        send_parts(
            t, 1, box.at[pl.ds(there, 1)], box_stat.at[pl.ds(there, 1)],
            (out_send.at[here], box_recv.at[there]), (stat_send.at[here], box_stat_recv.at[there]), t,
        )

    attend_second(SECOND[0])
    send_parts(
        HALF, 1, half, half_stat, (out_send.at[4], half_recv.at[0]),
        (stat_send.at[4], half_recv.at[1]), RELAY,
    )
    send_pair(2)
    send_pair(-2)
    attend_second(SECOND[1])
    send_pair(1)
    send_pair(-1)
    attend_first(FIRST[1], range(XS))
    attend_first(FIRST[0], range(XS))
    for t in NEAR:
        send_near(t)

    def send_final(number, offset, k):
        there = lax.rem(head + k, hs)
        device = (x * ZS + z_at(offset), there)
        send(
            final.at[number, pl.ds(there * own, own)], last.at[number, head],
            last_send.at[number, k], last_recv.at[number, head], device,
        )
        send(
            final_stat.at[number], last_stat.at[number, head],
            last_stat_send.at[number, k], last_stat_recv.at[number, head], device,
        )

    for i in range(len(NEAR)):
        arrived(pair.at[i], pair_recv.at[i])
        arrived(pair_stat.at[i], pair_stat_recv.at[i])
    for number, d in enumerate((-FAR, FAR)):
        terms = [(part[at_slot[d]], part_stat[at_slot[d]])]
        terms += [(pair[i, number], pair_stat[i, number]) for i in range(len(NEAR))]
        if d == FAR:
            arrived(half, half_recv.at[0])
            arrived(half_stat, half_recv.at[1])
            terms.append((half[0], half_stat[0]))
        merged, stat = merge(diagonal, terms)
        final[1 + number] = merged.astype(BF16).reshape(rows, group, HEAD_DIM)
        final_stat[1 + number] = stat
        for k in sorted(range(hs), key=lambda k: -min(k, hs - k)):
            send_final(1 + number, d, k)
    terms = [(part[at_slot[0]], part_stat[at_slot[0]])]
    for i in range(len(NEAR)):
        arrived(box.at[i], box_recv.at[i])
        arrived(box_stat.at[i], box_stat_recv.at[i])
        terms.append((box[i], box_stat[i]))
    merged, stat = merge(diagonal, terms)
    final[0] = merged.astype(BF16).reshape(rows, group, HEAD_DIM)
    final_stat[0] = stat
    for k in range(1, hs):
        send_final(0, 0, k)
    last[0, head] = final[0, pl.ds(head * own, own)]
    last_stat[0, head] = stat
    for copy in sent:
        copy.wait_send()
    for number in range(3):
        for k in range(0 if number else 1, hs):
            there = lax.rem(head + k, hs)
            arrived(last.at[number, there], last_recv.at[number, there])
            arrived(last_stat.at[number, there], last_stat_recv.at[number, there])
    mine = (own * group, HEAD_DIM)
    diagonal = (
        lax.broadcasted_iota(jnp.int32, mine, 0) + head * own * group
        == lax.broadcasted_iota(jnp.int32, mine, 1)
    )
    for g in range(hs):
        terms = [(last[number, g].reshape(mine), last_stat[number, g]) for number in range(3)]
        heads[g] = merge(diagonal, terms)[0]
    for i in range(own):
        pieces = [heads[g, i * group + h:i * group + h + 1, :] for g in range(hs) for h in range(group)]
        out_ref[i:i + 1, :] = jnp.concatenate(pieces, axis=1).astype(BF16)


def local(hs, prefix_len, page_slot, queries, new_kv, cache):
    rows = queries.shape[0]
    group = queries.shape[1] // HEAD_DIM
    block = rows * group
    own = rows // hs
    near = len(NEAR)
    dma = pltpu.SemaphoreType.DMA
    return pl.pallas_call(
        functools.partial(kernel, hs, rows, group),
        out_shape=jax.ShapeDtypeStruct((rows // hs, hs * group * HEAD_DIM), BF16),
        in_specs=[pl.BlockSpec(memory_space=pltpu.HBM)] * 5,
        out_specs=pl.BlockSpec(memory_space=pltpu.VMEM),
        scratch_shapes=[
            pltpu.SMEM(prefix_len.shape, jnp.int32),
            pltpu.VMEM(page_slot.shape, jnp.int32),
            pltpu.VMEM(queries.shape, BF16),
            pltpu.VMEM((XS, 2, SLOTS, PAGE, HEAD_DIM), BF16),
            pltpu.VMEM((XS, 2, rows, HEAD_DIM), BF16),
            pltpu.VMEM((ZS, block, HEAD_DIM), BF16),
            pltpu.VMEM((ZS, block, HEAD_DIM), BF16),
            pltpu.VMEM((ZS, 1, HEAD_DIM), F32),
            pltpu.VMEM((near, block, HEAD_DIM), BF16),
            pltpu.VMEM((near, 1, HEAD_DIM), F32),
            pltpu.VMEM((near, 2, block, HEAD_DIM), BF16),
            pltpu.VMEM((near, 2, 1, HEAD_DIM), F32),
            pltpu.VMEM((1, block, HEAD_DIM), BF16),
            pltpu.VMEM((1, 1, HEAD_DIM), F32),
            pltpu.VMEM((3, rows, group, HEAD_DIM), BF16),
            pltpu.VMEM((3, 1, HEAD_DIM), F32),
            pltpu.VMEM((3, hs, own, group, HEAD_DIM), BF16),
            pltpu.VMEM((3, hs, 1, HEAD_DIM), F32),
            pltpu.VMEM((ZS, block, HEAD_DIM), F32),
            pltpu.VMEM((ZS, block, 2 * HEAD_DIM), F32),
            pltpu.VMEM((XS * SLOTS, PAGE), F32),
            pltpu.VMEM((block, HEAD_DIM), F32),
            pltpu.VMEM((hs, own * group, HEAD_DIM), F32),
            dma((5,)), dma((6,)), dma((XS, SLOTS)), dma((XS,)), dma((XS,)), dma((ZS,)), dma((ZS,)),
            dma((near + 1,)), dma((near + 1,)), dma((near,)), dma((near,)), dma((near,)),
            dma((near,)), dma((near,)), dma((near,)), dma((2,)),
            dma((3, hs)), dma((3, hs)), dma((3, hs)), dma((3, hs)),
        ],
        compiler_params=pltpu.CompilerParams(
            collective_id=0, has_side_effects=True, vmem_limit_bytes=48 * 2**20
        ),
    )(*[pltpu.with_memory_space_constraint(a, pltpu.HBM) for a in (prefix_len, page_slot, queries, new_kv, cache.reshape(2, SLOTS, PAGE, HEAD_DIM))])


def solution(mesh):
    return jax.shard_map(
        functools.partial(local, mesh.shape["head"]),
        mesh=mesh,
        in_specs=(P(), P(), P("ctx", "head"), P(None, "ctx", "head"), P(None, "ctx", None, "head")),
        out_specs=P(("ctx", "head"), None),
        check_vma=False,
    )
```
